32 devices in a mesh: gx: 4 (over y, core), gy: 4 (over z), gz: 2 (over x).
Axes of the slice: x: 2, y: 2, z: 4, core: 2. Of those that a mesh axis runs over, the one named last changes fastest.
Arguments:
- phase: float32 [8, 64, 64, 256], P(None, 'gx', 'gy', 'gz'), may hold values from 0 to 1
- displacement: float32 [3, 64, 64, 256], P(None, 'gx', 'gy', 'gz'), may hold values from -2 to 2
- slot_ids: int32 [8, 4, 4, 16], P(None, 'gx', 'gy', 'gz'), may hold values from 0 to 256, as said below
- grain_variant: int32 [256], replicated, may hold values from 0 to 11
- variant_strain: float32 [12], replicated, may hold values from -0.3 to 0.3
Outputs:
- new_phases: float32 [8, 64, 64, 256], P(None, 'gx', 'gy', 'gz')
- new_displacement: float32 [3, 64, 64, 256], P(None, 'gx', 'gy', 'gz')
The draws below stay inside these ranges and needn't reach their ends.
Inputs may be any that keep to these rules, and one draw needn't show every extreme that they name: `slot_ids`: the 8 slots of a block hold distinct grain numbers, or 256 for an empty slot; a grain appears only in blocks that lie within one block of each other along every dimension, counted periodically.
All inputs are finite; a program needn't handle non-finite values.
Results may differ from the reference program's by a relative error of at most 0.0001.
Values sent between devices are 32-bit elements; how exact they have to be, the bound alone decides.
No kernel may reach another device: no remote copies, remote signals or barrier semaphores. Data moves between devices by JAX's collectives and lax.ppermute only.
A program may use at most 64 MiB of HBM per device.

```python
import jax
import jax.numpy as jnp
from jax import lax

SLOTS = 8
BLK = 16
VARIANTS = 12
STEPS = 2
SWEEPS = 2
NX = 64
NY = 64
NZ = 256
GRAINS = 256


def draw_slot_ids(key, part):
    blocks_x = NX // BLK
    blocks_y = NY // BLK
    blocks_z = NZ // BLK
    grains = blocks_x * blocks_y * blocks_z
    key_label, key_empty, key_order = jax.random.split(key, 3)
    index_x = jnp.arange(blocks_x, dtype=jnp.int32)[:, None, None]
    index_y = jnp.arange(blocks_y, dtype=jnp.int32)[None, :, None]
    index_z = jnp.arange(blocks_z, dtype=jnp.int32)[None, None, :]
    lists = []
    for offset_x in (0, 1):
        for offset_y in (0, 1):
            for offset_z in (0, 1):
                number = (index_x + offset_x) % blocks_x * blocks_y * blocks_z + (index_y + offset_y) % blocks_y * blocks_z + (index_z + offset_z) % blocks_z
                lists.append(jnp.broadcast_to(number, (blocks_x, blocks_y, blocks_z)))
    numbers = jnp.stack(lists)
    relabel = jax.random.permutation(key_label, grains).astype(jnp.int32)
    numbers = relabel[numbers]
    vacant = jax.random.randint(key_empty, numbers.shape, 0, 4) == 0
    numbers = jnp.where(vacant, grains, numbers)
    scores = jax.random.randint(key_order, numbers.shape, 0, 1 << 20) * 8 + jnp.arange(SLOTS, dtype=jnp.int32)[:, None, None, None]
    order = jnp.argsort(scores, axis=0)
    return jnp.take_along_axis(numbers, order, axis=0).astype(jnp.int32)


def set_ends(entries, own_key, low, top_value):
    longest = entries.shape.index(max(entries.shape))
    spots = []
    for shift in (0, 1):
        where = [jax.random.randint(jax.random.fold_in(own_key, axis), (), 0, length) for axis, length in enumerate(entries.shape)]
        where[longest] = (where[longest] + shift) % entries.shape[longest]
        spots.append(tuple(where))
    return entries.at[spots[0]].set(low).at[spots[1]].set(top_value)


def shard_levels(stream_key, shape, cuts, low, largest):
    level, own = 1.0, jax.random.fold_in(stream_key, 6)
    for dim, blocks in cuts:
        draws = jnp.exp(jax.random.uniform(jax.random.fold_in(own, dim), (blocks,), jnp.float32, low / len(cuts), largest / len(cuts)))
        level = level * jnp.repeat(draws, shape[dim] // blocks).reshape([-1 if axis == dim else 1 for axis in range(len(shape))])
    return level


def bell_draw(stream_key, dims, spread, most, cuts=(), kind=jnp.bfloat16):
    factor_of = shard_levels(stream_key, dims, cuts, -0.22, 0.18) if cuts else 1.0
    entries = jax.random.normal(stream_key, dims, jnp.float32) * spread * factor_of
    return jnp.minimum(jnp.maximum(entries, -most), most).astype(kind)


def setup_inputs(seed: int = 0) -> dict:
    arg_keys = jax.random.split(jax.random.key(seed), 6)
    return {
        "phase": jnp.clip(1.0 * jax.random.uniform(arg_keys[0], (SLOTS, NX, NY, NZ), jnp.float32) ** shard_levels(arg_keys[0], (SLOTS, NX, NY, NZ), ((1, 4), (2, 4), (3, 2)), -0.2, 0.2), 0.0, 1.0),
        "displacement": bell_draw(arg_keys[1], (3, NX, NY, NZ), 0.3, 2.0, ((1, 4), (2, 4), (3, 2)), jnp.float32),
        "slot_ids": draw_slot_ids(jax.random.fold_in(arg_keys[5], 71), 0),
        "grain_variant": set_ends(jax.random.randint(arg_keys[3], (GRAINS,), 0, VARIANTS), jax.random.fold_in(arg_keys[3], 1), 0, VARIANTS - 1).astype(jnp.int32),
        "variant_strain": jnp.clip(jax.random.uniform(arg_keys[4], (VARIANTS,), jnp.float32, -0.3, 0.3), -0.3, 0.3),
    }


well_linear = 1.0
well_cubic = 1.0
cross_term = 1.5
gradient_energy = 2.0
time_step = 0.04
shear = 1.0
lame_first = 1.0
relax_step = 0.06
bulk_trace = 3.0 * lame_first + 2.0 * shear
directions = ((1, 0, 0), (0, 1, 0), (0, 0, 1))


def combine(first, second, scale_one, scale_two):
    return tuple(scale_one * a + scale_two * b for a, b in zip(first, second))


def expand(blocks):
    c, bx, by, bz = blocks.shape
    big = jnp.broadcast_to(blocks[:, :, None, :, None, :, None], (c, bx, BLK, by, BLK, bz, BLK))
    return big.reshape(c, bx * BLK, by * BLK, bz * BLK)


def translate(neighbour, own_ids, near_ids, axis, sign, empty):
    c, nx, ny, nz = neighbour.shape
    bx, by, bz = own_ids.shape[1:]
    cube = neighbour.reshape(c, bx, BLK, by, BLK, bz, BLK)
    local = 2 * axis
    keep = BLK - 1 if sign > 0 else 0
    layer = lax.index_in_dim(cube, keep, local, keepdims=True)
    match = ((own_ids[:, None] == near_ids[None, :]) & (own_ids[:, None] < empty)).astype(neighbour.dtype)
    match = match[:, :, :, None, :, None, :, None]
    moved = jnp.sum(match * layer[None], axis=1)
    if sign > 0:
        rest = lax.slice_in_dim(cube, 0, BLK - 1, axis=local)
        cube = jnp.concatenate([rest, moved], axis=local)
    else:
        rest = lax.slice_in_dim(cube, 1, BLK, axis=local)
        cube = jnp.concatenate([moved, rest], axis=local)
    return cube.reshape(c, nx, ny, nz)


def divergence(sample, base):
    total = 0.0
    for i in range(3):
        unit = directions[i]
        minus = combine(unit, unit, -1, 0)
        total = total + 0.5 * (sample(base + i, unit) - sample(base + i, minus))
    return total


def stress_div(sample):
    zero = (0, 0, 0)
    result = []
    for i in range(3):
        unit = directions[i]
        minus = combine(unit, unit, -1, 0)
        centre = sample(i, zero)
        laplace = -6.0 * centre
        for j in range(3):
            other = directions[j]
            laplace = laplace + sample(i, other) + sample(i, combine(other, other, -1, 0))
        grad_div = 0.0
        for j in range(3):
            if j == i:
                grad_div = grad_div + sample(j, unit) - 2.0 * sample(j, zero) + sample(j, minus)
            else:
                other = directions[j]
                grad_div = grad_div + 0.25 * (sample(j, combine(unit, other, 1, 1)) - sample(j, combine(unit, other, 1, -1))
                                              - sample(j, combine(unit, other, -1, 1)) + sample(j, combine(unit, other, -1, -1)))
        grad_eps = 0.5 * (sample(3, unit) - sample(3, minus))
        result.append(centre + relax_step * (shear * laplace + (lame_first + shear) * grad_div - bulk_trace * grad_eps))
    return jnp.stack(result)


def phase_step(phases, laplace, dilation, strain):
    eigen = jnp.sum(phases * phases * strain, axis=0)
    trace = bulk_trace * (dilation - 3.0 * eigen)
    total = jnp.sum(phases * phases, axis=0)
    force = (-well_linear * phases + well_cubic * phases * phases * phases
             + 2.0 * cross_term * phases * (total - phases * phases)
             - gradient_energy * laplace - 2.0 * trace * strain * phases)
    return phases - time_step * force


def reference(phase, displacement, slot_ids, grain_variant, variant_strain):
    table = jnp.concatenate([variant_strain[grain_variant], jnp.zeros((1,), variant_strain.dtype)])
    strain = expand(table[slot_ids])
    active = expand((slot_ids < GRAINS).astype(phase.dtype))
    phases = phase * active
    shifts = displacement
    for step in range(STEPS):
        laplace = -6.0 * phases
        for axis in (1, 2, 3):
            for sign in (1, -1):
                laplace = laplace + translate(jnp.roll(phases, -sign, axis=axis), slot_ids,
                                              jnp.roll(slot_ids, -sign, axis=axis), axis, sign, GRAINS)

        def probe_shift(c, d, field=shifts):
            return jnp.roll(field[c], (-d[0], -d[1], -d[2]), axis=(0, 1, 2))

        dilation = divergence(probe_shift, 0)
        phases = phase_step(phases, laplace, dilation, strain)
        eigen = jnp.sum(phases * phases * strain, axis=0)
        for sweep in range(SWEEPS):
            field = jnp.concatenate([shifts, eigen[None]], axis=0)

            def probe_field(c, d, source=field):
                return jnp.roll(source[c], (-d[0], -d[1], -d[2]), axis=(0, 1, 2))

            shifts = stress_div(probe_field)
    return phases, shifts
```

```python
import functools

import jax
import jax.numpy as jnp
from jax import lax
from jax.experimental import pallas as pl
from jax.experimental.pallas import tpu as pltpu
from jax.sharding import PartitionSpec as P

SLOTS = 8
BLK = 16
STEPS = 2
SWEEPS = 2

well_linear = 1.0
well_cubic = 1.0
cross_term = 1.5
gradient_energy = 2.0
time_step = 0.04
shear = 1.0
lame_first = 1.0
relax_step = 0.06
bulk_trace = 3.0 * lame_first + 2.0 * shear

LANES = 128
PLANE = BLK * BLK
PITCH = 40
TOP = 8
REACH = 3
WIDE = BLK + 2 * REACH
OWN_Y = TOP + REACH
TALL = 24
FACE = SLOTS * BLK

f32 = jnp.float32


def lane_of(shape):
    return lax.broadcasted_iota(jnp.int32, shape, len(shape) - 1)


def roll(value, shift):
    if isinstance(shift, int):
        shift = shift % LANES
        if shift == 0:
            return value
    else:
        shift = lax.rem(shift + 2 * LANES, LANES)
    return pltpu.roll(value, shift, axis=value.ndim - 1)


def grow(ids):
    lane = lane_of((SLOTS, LANES)) // BLK
    out = jnp.zeros((SLOTS, LANES), f32)
    values = ids.astype(f32)
    for b in range(LANES // BLK):
        out = jnp.where(lane == b, jnp.broadcast_to(values[:, b : b + 1], (SLOTS, LANES)), out)
    return out


def fold_faces(first0, first1, last0, last1):
    lane = lane_of(first0.shape)
    return jnp.where(
        lane < BLK,
        first0,
        jnp.where(
            lane < 2 * BLK,
            roll(first1, BLK),
            jnp.where(lane < LANES - BLK, roll(last1, -BLK), last0),
        ),
    )


def start_kernel(ph, dp, ids, xlo, xhi, ylo, yhi, zm, pk):
    numbers = grow(ids[...])
    for s in range(SLOTS):
        rows = pl.ds(s * BLK, BLK)
        xlo[rows, :] = ph[pl.ds(s * PLANE, BLK), :]
        xhi[rows, :] = ph[pl.ds(s * PLANE + PLANE - BLK, BLK), :]
        ylo[rows, :] = ph[pl.ds(s * PLANE, BLK, stride=BLK), :]
        yhi[rows, :] = ph[pl.ds(s * PLANE + BLK - 1, BLK, stride=BLK), :]
    rows = pl.ds(FACE, BLK)
    xlo[rows, :] = dp[pl.ds(0, BLK), :]
    xhi[rows, :] = dp[pl.ds(PLANE - BLK, BLK), :]
    ylo[rows, :] = dp[pl.ds(PLANE, BLK, stride=BLK), :]
    yhi[rows, :] = dp[pl.ds(PLANE + BLK - 1, BLK, stride=BLK), :]
    for ref in (xlo, xhi, ylo, yhi):
        ref[pl.ds(FACE + BLK, SLOTS), :] = numbers
    zm[pl.ds(FACE // 2 + 8, SLOTS), :] = numbers
    spot = lane_of((8, LANES)) % BLK
    for f in range(SLOTS + 1):
        packs = []
        for half in range(2):
            first = jnp.zeros((8, LANES), f32)
            last = jnp.zeros((8, LANES), f32)
            for x in range(BLK):
                if f < SLOTS:
                    value = ph[pl.ds(f * PLANE + x * BLK + 8 * half, 8), :]
                else:
                    value = dp[pl.ds(2 * PLANE + x * BLK + 8 * half, 8), :]
                first = jnp.where(spot == x, roll(value, x), first)
                last = jnp.where(spot == x, roll(value, x - BLK + 1), last)
            packs.append((first, last))
            if f < SLOTS:
                pk[0, f, pl.ds(8 * half, 8), :] = first
                pk[1, f, pl.ds(8 * half, 8), :] = last
        zm[pl.ds(f * 8, 8), :] = fold_faces(packs[0][0], packs[1][0], packs[0][1], packs[1][1])


def update_phases(load, pp, mk, st, faces, pk, dil, out, e_out, pk_out, mv):
    xm, xp, ym, yp, zl, zr = faces
    lane = lane_of((8, LANES))
    spot = lane % BLK

    def fill(x, _):
        for s in range(SLOTS):
            pp[s, x + 1, pl.ds(8, BLK), :] = load(s, x)
        return 0

    lax.fori_loop(0, BLK, fill, 0)

    def match(direction, s, layers):
        total = None
        for t in range(SLOTS):
            term = mk[direction, s, pl.ds(t, 1), :] * layers[t]
            total = term if total is None else total + term
        return total

    for direction, face, place in ((0, xm, 0), (1, xp, BLK + 1)):
        layers = [face(t) for t in range(SLOTS)]
        for s in range(SLOTS):
            pp[s, place, pl.ds(8, BLK), :] = match(direction, s, layers)
    for direction, face, place in ((2, ym, 7), (3, yp, 8 + BLK)):
        layers = [face(t) for t in range(SLOTS)]
        for s in range(SLOTS):
            moved = match(direction, s, layers)
            for x in range(BLK):
                pp[s, x + 1, pl.ds(place, 1), :] = moved[x : x + 1, :]
    for half in range(2):
        rows = pl.ds(8 * half, 8)
        before = [
            jnp.where(lane < BLK, roll(zl(t), BLK * (1 + half)), roll(pk[1, t, rows, :], BLK))
            for t in range(SLOTS)
        ]
        for s in range(SLOTS):
            mv[0, s, rows, :] = match(4, s, before)
        after = [
            jnp.where(
                lane >= LANES - BLK, roll(zr(t), -BLK * (1 + half)), roll(pk[0, t, rows, :], -BLK)
            )
            for t in range(SLOTS)
        ]
        for s in range(SLOTS):
            mv[1, s, rows, :] = match(5, s, after)

    if pk_out is not None:
        pk_out[...] = jnp.zeros(pk_out.shape, f32)

    def layer(x, _):
        for half in range(2):
            r0 = 8 + 8 * half
            rows = pl.ds(8 * half, 8)
            values = [pp[s, x + 1, pl.ds(r0, 8), :] for s in range(SLOTS)]
            total = None
            eigen = None
            for s in range(SLOTS):
                square = values[s] * values[s]
                part = square * st[pl.ds(s, 1), :]
                total = square if total is None else total + square
                eigen = part if eigen is None else eigen + part
            trace = bulk_trace * (dil[x, rows, :] - 3.0 * eigen)
            base = (1.0 + time_step * well_linear - 6.0 * time_step * gradient_energy) - (
                2.0 * cross_term * time_step
            ) * total
            pull = (2.0 * time_step) * trace
            fresh = None
            for s in range(SLOTS):
                p = values[s]
                after = jnp.where(
                    spot == BLK - 1, roll(mv[1, s, rows, :], BLK - 1 - x), roll(p, -1)
                )
                before = jnp.where(spot == 0, roll(mv[0, s, rows, :], -x), roll(p, 1))
                near = (
                    (pp[s, x, pl.ds(r0, 8), :] + pp[s, x + 2, pl.ds(r0, 8), :])
                    + (pp[s, x + 1, pl.ds(r0 - 1, 8), :] + pp[s, x + 1, pl.ds(r0 + 1, 8), :])
                    + (after + before)
                )
                rate = (
                    base
                    + (time_step * (2.0 * cross_term - well_cubic)) * (p * p)
                    + pull * st[pl.ds(s, 1), :]
                )
                new = p * rate + (time_step * gradient_energy) * near
                out[pl.ds(pl.multiple_of(s * PLANE + x * BLK + 8 * half, 8), 8), :] = new
                part = new * new * st[pl.ds(s, 1), :]
                fresh = part if fresh is None else fresh + part
                if pk_out is not None:
                    pk_out[0, s, rows, :] = jnp.where(
                        spot == x, roll(new, x), pk_out[0, s, rows, :]
                    )
                    pk_out[1, s, rows, :] = jnp.where(
                        spot == x, roll(new, x - BLK + 1), pk_out[1, s, rows, :]
                    )
            e_out[pl.ds(pl.multiple_of(x * BLK + 8 * half, 8), 8), :] = fresh
        return 0

    lax.fori_loop(0, BLK, layer, 0)


def first_kernel(
    ids_s, variant_s, strain_s, ids, ph, dp, pk, xm, xp, ym, yp, zl, zr,
    out, e_out, pk_out, zphase, xlo, xhi, mk, st, pp, dil, mv, act,
):
    grains = variant_s.shape[0]
    own = grow(ids[...])
    lane = lane_of((SLOTS, LANES))
    owner = lane_of((1, LANES)) // BLK
    for s in range(SLOTS):
        row = jnp.zeros((1, LANES), f32)
        live = jnp.zeros((1, LANES), f32)
        for b in range(LANES // BLK):
            number = ids_s[s, b]
            value = strain_s[variant_s[jnp.minimum(number, grains - 1)]]
            row = jnp.where(owner == b, jnp.where(number < grains, value, 0.0), row)
            live = jnp.where(owner == b, jnp.where(number < grains, 1.0, 0.0), live)
        st[pl.ds(s, 1), :] = row
        act[pl.ds(s, 1), :] = live
    tail = pl.ds(FACE + BLK, SLOTS)
    ztail = pl.ds(FACE // 2 + 8, SLOTS)
    beside = [xm[tail, :], xp[tail, :], ym[tail, :], yp[tail, :]]
    beside.append(jnp.where(lane < BLK, roll(zl[ztail, :], BLK), roll(own, BLK)))
    beside.append(jnp.where(lane >= LANES - BLK, roll(zr[ztail, :], -BLK), roll(own, -BLK)))
    for direction in range(6):
        for s in range(SLOTS):
            mine = own[s : s + 1, :]
            mk[direction, s] = jnp.where(
                (mine == beside[direction]) & (mine < float(grains)), 1.0, 0.0
            )

    lane2 = lane_of((BLK, LANES))
    row2 = lax.broadcasted_iota(jnp.int32, (BLK, LANES), 0)
    urow = pl.ds(FACE, BLK)
    wrow = pl.ds(FACE // 2, 8)
    wl = zl[wrow, :]
    wr = zr[wrow, :]
    for x in range(BLK):
        up = xp[urow, :] if x == BLK - 1 else dp[pl.ds((x + 1) * BLK, BLK), :]
        down = xm[urow, :] if x == 0 else dp[pl.ds((x - 1) * BLK, BLK), :]
        v = dp[pl.ds(PLANE + x * BLK, BLK), :]
        vp = jnp.where(row2 == BLK - 1, yp[pl.ds(FACE + x, 1), :], pltpu.roll(v, BLK - 1, axis=0))
        vm = jnp.where(row2 == 0, ym[pl.ds(FACE + x, 1), :], pltpu.roll(v, 1, axis=0))
        w = dp[pl.ds(2 * PLANE + x * BLK, BLK), :]
        right = jnp.concatenate([roll(wr, LANES - 1 - x), roll(wr, LANES - 1 - BLK - x)], axis=0)
        left = jnp.concatenate([roll(wl, BLK - x), roll(wl, 2 * BLK - x)], axis=0)
        wp = jnp.where(lane2 == LANES - 1, right, roll(w, -1))
        wm = jnp.where(lane2 == 0, left, roll(w, 1))
        dil[x] = 0.5 * ((up - down) + (vp - vm) + (wp - wm))

    def load(s, x):
        rows = pl.ds(pl.multiple_of(s * PLANE + x * BLK, BLK), BLK)
        return ph[rows, :] * act[pl.ds(s, 1), :]

    faces = (
        lambda t: xm[pl.ds(t * BLK, BLK), :],
        lambda t: xp[pl.ds(t * BLK, BLK), :],
        lambda t: ym[pl.ds(t * BLK, BLK), :],
        lambda t: yp[pl.ds(t * BLK, BLK), :],
        lambda t: zl[pl.ds(t * 8, 8), :],
        lambda t: zr[pl.ds(t * 8, 8), :],
    )
    update_phases(load, pp, mk, st, faces, pk, dil, out, e_out, pk_out, mv)
    for s in range(SLOTS):
        low, high = pl.ds(0, 8), pl.ds(8, 8)
        zphase[pl.ds(s * 8, 8), :] = fold_faces(
            pk_out[0, s, low, :], pk_out[0, s, high, :], pk_out[1, s, low, :], pk_out[1, s, high, :]
        )
    halo = REACH
    fields = field_rows(dp, e_out)
    x_sides(fields, halo, xlo, xhi)
    for s in range(SLOTS):
        rows = pl.ds(4 * halo * BLK + s * BLK, BLK)
        xlo[rows, :] = out[pl.ds(s * PLANE, BLK), :]
        xhi[rows, :] = out[pl.ds(s * PLANE + PLANE - BLK, BLK), :]


def field_rows(dp, e):
    def rows(f, x, y, n):
        if f < 3:
            return dp[pl.ds(f * PLANE + x * BLK + y, n), :]
        return e[pl.ds(x * BLK + y, n), :]

    return rows


def x_sides(fields, halo, xlo, xhi):
    for f in range(4):
        for k in range(halo):
            rows = pl.ds((f * halo + k) * BLK, BLK)
            xlo[rows, :] = fields(f, k, 0, BLK)
            xhi[rows, :] = fields(f, BLK - halo + k, 0, BLK)


def extended_rows(fields, xm, xp, halo):
    def rows(f, i, y, n):
        if i < halo:
            return xm[pl.ds((f * halo + i) * BLK + y, n), :]
        if i >= halo + BLK:
            return xp[pl.ds((f * halo + i - halo - BLK) * BLK + y, n), :]
        return fields(f, i - halo, y, n)

    return rows


def y_kernel(halo, with_phases, *refs):
    if with_phases:
        dp, e, xm, xp, ph, ylo, yhi = refs
    else:
        dp, e, xm, xp, ylo, yhi = refs
    rows = extended_rows(field_rows(dp, e), xm, xp, halo)
    count = BLK + 2 * halo
    for f in range(4):
        for i in range(count):
            place = pl.ds((f * count + i) * halo, halo)
            ylo[place, :] = rows(f, i, 0, halo)
            yhi[place, :] = rows(f, i, BLK - halo, halo)
    if with_phases:
        for s in range(SLOTS):
            place = pl.ds(4 * count * halo + s * BLK, BLK)
            ylo[place, :] = ph[pl.ds(s * PLANE, BLK, stride=BLK), :]
            yhi[place, :] = ph[pl.ds(s * PLANE + BLK - 1, BLK, stride=BLK), :]


def pack_width(halo):
    return 8 if halo > 2 else 4


def z_kernel(halo, with_phases, *refs):
    if with_phases:
        dp, e, xm, xp, ym, yp, zphase, zm, field = refs
    else:
        dp, e, xm, xp, ym, yp, zm, field = refs
    rows = extended_rows(field_rows(dp, e), xm, xp, halo)
    count = BLK + 2 * halo
    skip = REACH - halo
    width = pack_width(halo)
    per = LANES // width
    groups = -(-count // per)
    lane = lane_of((TALL, LANES))
    spot = lane // width
    low = lane % width < width // 2
    for f in range(4):
        packs = [jnp.zeros((TALL, LANES), f32) for _ in range(groups)]
        for i in range(count):
            field[f, i + skip, pl.ds(OWN_Y, BLK), :] = rows(f, i, 0, BLK)
            side = pl.ds((f * count + i) * halo, halo)
            field[f, i + skip, pl.ds(OWN_Y - halo, halo), :] = ym[side, :]
            field[f, i + skip, pl.ds(OWN_Y + BLK, halo), :] = yp[side, :]
            value = field[f, i + skip, pl.ds(TOP, TALL), :]
            g, k = i // per, i % per
            both = jnp.where(low, roll(value, width * k), roll(value, width * (k + 1)))
            packs[g] = jnp.where(spot == k, both, packs[g])
        for g in range(groups):
            zm[pl.ds((f * groups + g) * TALL, TALL), :] = packs[g]
    if with_phases:
        zm[pl.ds(4 * groups * TALL, FACE // 2), :] = zphase[...]


def shift_z(main, wing, sign):
    lane = lane_of(main.shape)
    rm, rw = roll(main, -sign), roll(wing, -sign)
    edge = lane == (LANES - 1 if sign > 0 else 0)
    return jnp.where(edge, rw, rm), jnp.where(edge, rm, rw)


def sweep(main, wing, em, ew, dst, xyz, first, stop):
    src = (main, wing)
    eps = (em, ew)

    def parts(i, t, kinds):
        r0 = TOP + 8 * t
        rows = pl.ds(r0, 8)
        wp = shift_z(main[2, i, rows, :], wing[2, i, rows, :], 1)
        wm = shift_z(main[2, i, rows, :], wing[2, i, rows, :], -1)
        for tile in range(2):
            ref = src[tile]
            b = ref[1, i, pl.ds(r0 + 1, 8), :] - ref[1, i, pl.ds(r0 - 1, 8), :]
            c = wp[tile] - wm[tile]
            e = (0.5 * bulk_trace) * eps[tile](i, rows)
            half = 0.5 * (lame_first + shear) * 0.5
            xyz[tile, 0, i, rows, :] = half * (b + c) - e
            if kinds > 1:
                a = ref[0, i + 1, rows, :] - ref[0, i - 1, rows, :]
                xyz[tile, 1, i, rows, :] = half * (a + c) - e
                xyz[tile, 2, i, rows, :] = half * (a + b) - e

    for t in range(TALL // 8):
        parts(first - 1, t, 1)
        parts(stop, t, 1)

    def collect(i, _):
        for t in range(TALL // 8):
            parts(i, t, 3)
        return 0

    lax.fori_loop(first, stop, collect, 0)
    own = shear + (lame_first + shear)
    centre = 6.0 * shear + 2.0 * (lame_first + shear)

    def apply(i, _):
        for t in range(TALL // 8):
            r0 = TOP + 8 * t
            rows = pl.ds(r0, 8)
            lift, drop = pl.ds(r0 + 1, 8), pl.ds(r0 - 1, 8)
            zp = shift_z(xyz[0, 2, i, rows, :], xyz[1, 2, i, rows, :], 1)
            zm = shift_z(xyz[0, 2, i, rows, :], xyz[1, 2, i, rows, :], -1)
            for k in range(3):
                here = (main[k, i, rows, :], wing[k, i, rows, :])
                fp = shift_z(here[0], here[1], 1)
                fm = shift_z(here[0], here[1], -1)
                for tile in range(2):
                    ref = src[tile]
                    pairs = [
                        ref[k, i + 1, rows, :] + ref[k, i - 1, rows, :],
                        ref[k, i, lift, :] + ref[k, i, drop, :],
                        fp[tile] + fm[tile],
                    ]
                    others = [pairs[j] for j in range(3) if j != k]
                    if k == 0:
                        push = xyz[tile, 0, i + 1, rows, :] - xyz[tile, 0, i - 1, rows, :]
                    elif k == 1:
                        push = xyz[tile, 1, i, lift, :] - xyz[tile, 1, i, drop, :]
                    else:
                        push = zp[tile] - zm[tile]
                    change = own * pairs[k] + shear * (others[0] + others[1]) + push
                    dst[tile, k, i, rows, :] = (
                        (1.0 - relax_step * centre) * here[tile] + relax_step * change
                    )
        return 0

    lax.fori_loop(first, stop, apply, 0)


def relax(halo, field, zl, zr, wing, mid, end, xyz):
    count = BLK + 2 * halo
    skip = REACH - halo
    width = pack_width(halo)
    per = LANES // width
    groups = -(-count // per)
    lane = lane_of((TALL, LANES))
    for f in range(4):
        for i in range(count):
            g, k = i // per, i % per
            rows = pl.ds((f * groups + g) * TALL, TALL)
            wing[f, i + skip, pl.ds(TOP, TALL), :] = jnp.where(
                lane < LANES // 2,
                roll(zr[rows, :], -width * k),
                roll(zl[rows, :], -width * (k + 1)),
            )
    first, stop = skip + 1, skip + count - 1
    em = lambda i, rows: field[3, i, rows, :]
    ew = lambda i, rows: wing[3, i, rows, :]
    sweep(field, wing, em, ew, mid, xyz, first, stop)
    sweep(mid.at[0], mid.at[1], em, ew, end, xyz, first + 1, stop - 1)


def second_kernel(
    field, zl, zr, ph, pk, mk, st, xm, xp, ym, yp,
    out, e_out, moved, xlo, xhi, wing, mid, end, xyz, pp, dil, mv,
):
    halo = REACH
    relax(halo, field, zl, zr, wing, mid, end, xyz)
    own = pl.ds(OWN_Y, BLK)

    def strain_rate(x, _):
        i = x + REACH
        wp = shift_z(end[0, 2, i, own, :], end[1, 2, i, own, :], 1)[0]
        wm = shift_z(end[0, 2, i, own, :], end[1, 2, i, own, :], -1)[0]
        dil[x] = 0.5 * (
            (end[0, 0, i + 1, own, :] - end[0, 0, i - 1, own, :])
            + (end[0, 1, i, pl.ds(OWN_Y + 1, BLK), :] - end[0, 1, i, pl.ds(OWN_Y - 1, BLK), :])
            + (wp - wm)
        )
        for k in range(3):
            moved[pl.ds(pl.multiple_of(k * PLANE + x * BLK, BLK), BLK), :] = end[0, k, i, own, :]
        return 0

    lax.fori_loop(0, BLK, strain_rate, 0)
    count = BLK + 2 * halo
    xbase = 4 * halo * BLK
    ybase = 4 * count * halo
    zbase = 4 * (-(-count // (LANES // pack_width(halo)))) * TALL

    def load(s, x):
        return ph[pl.ds(pl.multiple_of(s * PLANE + x * BLK, BLK), BLK), :]

    faces = (
        lambda t: xm[pl.ds(xbase + t * BLK, BLK), :],
        lambda t: xp[pl.ds(xbase + t * BLK, BLK), :],
        lambda t: ym[pl.ds(ybase + t * BLK, BLK), :],
        lambda t: yp[pl.ds(ybase + t * BLK, BLK), :],
        lambda t: zl[pl.ds(zbase + t * 8, 8), :],
        lambda t: zr[pl.ds(zbase + t * 8, 8), :],
    )
    update_phases(load, pp, mk, st, faces, pk, dil, out, e_out, None, mv)
    x_sides(field_rows(moved, e_out), SWEEPS, xlo, xhi)


def last_kernel(field, zl, zr, moved, wing, mid, end, xyz):
    relax(SWEEPS, field, zl, zr, wing, mid, end, xyz)
    own = pl.ds(OWN_Y, BLK)

    def copy(x, _):
        for k in range(3):
            moved[pl.ds(pl.multiple_of(k * PLANE + x * BLK, BLK), BLK), :] = end[
                0, k, x + REACH, own, :
            ]
        return 0

    lax.fori_loop(0, BLK, copy, 0)


def rows_of(n):
    return jax.ShapeDtypeStruct((n, LANES), f32)


def call(kernel, outs, args, scratch=(), scalars=0, name=None):
    vmem = pl.BlockSpec(memory_space=pltpu.VMEM)
    smem = pl.BlockSpec(memory_space=pltpu.SMEM)
    return pl.pallas_call(
        kernel,
        out_shape=outs,
        in_specs=[smem] * scalars + [vmem] * (len(args) - scalars),
        out_specs=jax.tree.map(lambda _: vmem, outs),
        scratch_shapes=[pltpu.VMEM(shape, f32) for shape in scratch],
        name=name,
        compiler_params=pltpu.CompilerParams(vmem_limit_bytes=40 * 2**20),
    )(*args)


def swap(low, high, axis):
    n = lax.axis_size(axis)
    below = lax.ppermute(high, axis, [(i, (i + 1) % n) for i in range(n)])
    if low is high and n == 2:
        return below, below
    above = lax.ppermute(low, axis, [((i + 1) % n, i) for i in range(n)])
    return below, above


def local(phase, displacement, slot_ids, grain_variant, variant_strain):
    ph = phase.reshape(-1, LANES)
    dp = displacement.reshape(-1, LANES)
    ids = slot_ids.reshape(SLOTS, -1)
    side = rows_of(FACE + BLK + SLOTS)
    packed = jax.ShapeDtypeStruct((2, SLOTS, BLK, LANES), f32)
    padded = (SLOTS, BLK + 2, 32, LANES)
    square = (BLK, BLK, LANES)
    turned = (2, SLOTS, BLK, LANES)
    wide = (4, WIDE, PITCH, LANES)
    double = (2, 3, WIDE, PITCH, LANES)

    xlo, xhi, ylo, yhi, zm, pk = call(
        start_kernel,
        (side, side, side, side, rows_of(FACE // 2 + 8 + SLOTS), packed),
        (ph, dp, ids),
        name="start",
    )
    xm, xp = swap(xlo, xhi, "gx")
    ym, yp = swap(ylo, yhi, "gy")
    zl, zr = swap(zm, zm, "gz")

    halo = REACH
    count = BLK + 2 * halo
    groups = -(-count // (LANES // pack_width(halo)))
    xside = rows_of(4 * halo * BLK + FACE)
    phases, eigen, pk, zphase, xlo, xhi, mk, st = call(
        first_kernel,
        (
            rows_of(SLOTS * PLANE),
            rows_of(PLANE),
            packed,
            rows_of(FACE // 2),
            xside,
            xside,
            jax.ShapeDtypeStruct((6, SLOTS, SLOTS, LANES), f32),
            rows_of(SLOTS),
        ),
        (ids, grain_variant, variant_strain, ids, ph, dp, pk, xm, xp, ym, yp, zl, zr),
        scratch=(padded, square, turned, (SLOTS, LANES)),
        scalars=3,
        name="first",
    )
    xm, xp = swap(xlo, xhi, "gx")
    yside = rows_of(4 * count * halo + FACE)
    ylo, yhi = call(
        functools.partial(y_kernel, halo, True),
        (yside, yside),
        (dp, eigen, xm, xp, phases),
        name="rows_a",
    )
    ym, yp = swap(ylo, yhi, "gy")
    field_shape = jax.ShapeDtypeStruct(wide, f32)
    zm, field = call(
        functools.partial(z_kernel, halo, True),
        (rows_of(4 * groups * TALL + FACE // 2), field_shape),
        (dp, eigen, xm, xp, ym, yp, zphase),
        name="lanes_a",
    )
    zl, zr = swap(zm, zm, "gz")
    halo = SWEEPS
    count = BLK + 2 * halo
    groups = -(-count // (LANES // pack_width(halo)))
    xside = rows_of(4 * halo * BLK)
    phases, eigen, moved, xlo, xhi = call(
        second_kernel,
        (rows_of(SLOTS * PLANE), rows_of(PLANE), rows_of(3 * PLANE), xside, xside),
        (field, zl, zr, phases, pk, mk, st, xm, xp, ym, yp),
        scratch=(wide, double, double, double, padded, square, turned),
        name="second",
    )
    xm, xp = swap(xlo, xhi, "gx")
    yside = rows_of(4 * count * halo)
    ylo, yhi = call(
        functools.partial(y_kernel, halo, False),
        (yside, yside),
        (moved, eigen, xm, xp),
        name="rows_b",
    )
    ym, yp = swap(ylo, yhi, "gy")
    zm, field = call(
        functools.partial(z_kernel, halo, False),
        (rows_of(4 * groups * TALL), field_shape),
        (moved, eigen, xm, xp, ym, yp),
        name="lanes_b",
    )
    zl, zr = swap(zm, zm, "gz")
    moved = call(
        last_kernel,
        rows_of(3 * PLANE),
        (field, zl, zr),
        scratch=(wide, double, double, double),
        name="last",
    )
    return phases.reshape(phase.shape), moved.reshape(displacement.shape)


def solution(mesh):
    spec = P(None, "gx", "gy", "gz")
    return jax.shard_map(
        local,
        mesh=mesh,
        in_specs=(spec, spec, spec, P(), P()),
        out_specs=(spec, spec),
        check_vma=False,
    )
```

```python
import functools

import jax
import jax.numpy as jnp
from jax import lax
from jax.experimental import pallas as pl
from jax.experimental.pallas import tpu as pltpu
from jax.sharding import PartitionSpec as P

SLOTS = 8
BLK = 16
STEPS = 2
SWEEPS = 2

well_linear = 1.0
well_cubic = 1.0
cross_term = 1.5
gradient_energy = 2.0
time_step = 0.04
shear = 1.0
lame_first = 1.0
relax_step = 0.06
bulk_trace = 3.0 * lame_first + 2.0 * shear

LANES = 128
PLANE = BLK * BLK
PITCH = 40
TOP = 8
REACH = 3
WIDE = BLK + 2 * REACH
OWN_Y = TOP + REACH
TALL = 24
FACE = SLOTS * BLK

f32 = jnp.float32


def lane_of(shape):
    return lax.broadcasted_iota(jnp.int32, shape, len(shape) - 1)


def roll(value, shift):
    if isinstance(shift, int):
        shift = shift % LANES
        if shift == 0:
            return value
    else:
        shift = lax.rem(shift + 2 * LANES, LANES)
    return pltpu.roll(value, shift, axis=value.ndim - 1)


def grow(ids):
    lane = lane_of((SLOTS, LANES)) // BLK
    out = jnp.zeros((SLOTS, LANES), f32)
    values = ids.astype(f32)
    for b in range(LANES // BLK):
        out = jnp.where(lane == b, jnp.broadcast_to(values[:, b : b + 1], (SLOTS, LANES)), out)
    return out


def fold_faces(first0, first1, last0, last1):
    lane = lane_of(first0.shape)
    return jnp.where(
        lane < BLK,
        first0,
        jnp.where(
            lane < 2 * BLK,
            roll(first1, BLK),
            jnp.where(lane < LANES - BLK, roll(last1, -BLK), last0),
        ),
    )


def start_kernel(ph, dp, ids, xlo, xhi, ylo, yhi, zm, pk):
    numbers = grow(ids[...])
    for s in range(SLOTS):
        rows = pl.ds(s * BLK, BLK)
        xlo[rows, :] = ph[pl.ds(s * PLANE, BLK), :]
        xhi[rows, :] = ph[pl.ds(s * PLANE + PLANE - BLK, BLK), :]
        ylo[rows, :] = ph[pl.ds(s * PLANE, BLK, stride=BLK), :]
        yhi[rows, :] = ph[pl.ds(s * PLANE + BLK - 1, BLK, stride=BLK), :]
    rows = pl.ds(FACE, BLK)
    xlo[rows, :] = dp[pl.ds(0, BLK), :]
    xhi[rows, :] = dp[pl.ds(PLANE - BLK, BLK), :]
    ylo[rows, :] = dp[pl.ds(PLANE, BLK, stride=BLK), :]
    yhi[rows, :] = dp[pl.ds(PLANE + BLK - 1, BLK, stride=BLK), :]
    for ref in (xlo, xhi, ylo, yhi):
        ref[pl.ds(FACE + BLK, SLOTS), :] = numbers
    zm[pl.ds(FACE // 2 + 8, SLOTS), :] = numbers
    spot = lane_of((8, LANES)) % BLK
    for f in range(SLOTS + 1):
        packs = []
        for half in range(2):
            first = jnp.zeros((8, LANES), f32)
            last = jnp.zeros((8, LANES), f32)
            for x in range(BLK):
                if f < SLOTS:
                    value = ph[pl.ds(f * PLANE + x * BLK + 8 * half, 8), :]
                else:
                    value = dp[pl.ds(2 * PLANE + x * BLK + 8 * half, 8), :]
                first = jnp.where(spot == x, roll(value, x), first)
                last = jnp.where(spot == x, roll(value, x - BLK + 1), last)
            packs.append((first, last))
            if f < SLOTS:
                pk[0, f, pl.ds(8 * half, 8), :] = first
                pk[1, f, pl.ds(8 * half, 8), :] = last
        zm[pl.ds(f * 8, 8), :] = fold_faces(packs[0][0], packs[1][0], packs[0][1], packs[1][1])


def update_phases(load, pp, mk, st, faces, pk, dil, out, e_out, pk_out, mv):
    xm, xp, ym, yp, zl, zr = faces
    lane = lane_of((8, LANES))
    spot = lane % BLK

    def fill(x, _):
        for s in range(SLOTS):
            pp[s, x + 1, pl.ds(8, BLK), :] = load(s, x)
        return 0

    lax.fori_loop(0, BLK, fill, 0)

    def match(direction, s, layers):
        total = None
        for t in range(SLOTS):
            term = mk[direction, s, pl.ds(t, 1), :] * layers[t]
            total = term if total is None else total + term
        return total

    for direction, face, place in ((0, xm, 0), (1, xp, BLK + 1)):
        layers = [face(t) for t in range(SLOTS)]
        for s in range(SLOTS):
            pp[s, place, pl.ds(8, BLK), :] = match(direction, s, layers)
    for direction, face, place in ((2, ym, 7), (3, yp, 8 + BLK)):
        layers = [face(t) for t in range(SLOTS)]
        for s in range(SLOTS):
            moved = match(direction, s, layers)
            for x in range(BLK):
                pp[s, x + 1, pl.ds(place, 1), :] = moved[x : x + 1, :]
    for half in range(2):
        rows = pl.ds(8 * half, 8)
        before = [
            jnp.where(lane < BLK, roll(zl(t), BLK * (1 + half)), roll(pk[1, t, rows, :], BLK))
            for t in range(SLOTS)
        ]
        for s in range(SLOTS):
            mv[0, s, rows, :] = match(4, s, before)
        after = [
            jnp.where(
                lane >= LANES - BLK, roll(zr(t), -BLK * (1 + half)), roll(pk[0, t, rows, :], -BLK)
            )
            for t in range(SLOTS)
        ]
        for s in range(SLOTS):
            mv[1, s, rows, :] = match(5, s, after)

    if pk_out is not None:
        pk_out[...] = jnp.zeros(pk_out.shape, f32)

    def layer(x, _):
        for half in range(2):
            r0 = 8 + 8 * half
            rows = pl.ds(8 * half, 8)
            values = [pp[s, x + 1, pl.ds(r0, 8), :] for s in range(SLOTS)]
            total = None
            eigen = None
            for s in range(SLOTS):
                square = values[s] * values[s]
                part = square * st[pl.ds(s, 1), :]
                total = square if total is None else total + square
                eigen = part if eigen is None else eigen + part
            trace = bulk_trace * (dil[x, rows, :] - 3.0 * eigen)
            base = (1.0 + time_step * well_linear - 6.0 * time_step * gradient_energy) - (
                2.0 * cross_term * time_step
            ) * total
            pull = (2.0 * time_step) * trace
            fresh = None
            for s in range(SLOTS):
                p = values[s]
                after = jnp.where(
                    spot == BLK - 1, roll(mv[1, s, rows, :], BLK - 1 - x), roll(p, -1)
                )
                before = jnp.where(spot == 0, roll(mv[0, s, rows, :], -x), roll(p, 1))
                near = (
                    (pp[s, x, pl.ds(r0, 8), :] + pp[s, x + 2, pl.ds(r0, 8), :])
                    + (pp[s, x + 1, pl.ds(r0 - 1, 8), :] + pp[s, x + 1, pl.ds(r0 + 1, 8), :])
                    + (after + before)
                )
                rate = (
                    base
                    + (time_step * (2.0 * cross_term - well_cubic)) * (p * p)
                    + pull * st[pl.ds(s, 1), :]
                )
                new = p * rate + (time_step * gradient_energy) * near
                out[pl.ds(pl.multiple_of(s * PLANE + x * BLK + 8 * half, 8), 8), :] = new
                part = new * new * st[pl.ds(s, 1), :]
                fresh = part if fresh is None else fresh + part
                if pk_out is not None:
                    pk_out[0, s, rows, :] = jnp.where(
                        spot == x, roll(new, x), pk_out[0, s, rows, :]
                    )
                    pk_out[1, s, rows, :] = jnp.where(
                        spot == x, roll(new, x - BLK + 1), pk_out[1, s, rows, :]
                    )
            e_out[pl.ds(pl.multiple_of(x * BLK + 8 * half, 8), 8), :] = fresh
        return 0

    lax.fori_loop(0, BLK, layer, 0)


def first_kernel(
    ids_s, variant_s, strain_s, ids, ph, dp, pk, xm, xp, ym, yp, zl, zr,
    out, e_out, pk_out, zphase, xlo, xhi, mk, st, pp, dil, mv, act,
):
    grains = variant_s.shape[0]
    own = grow(ids[...])
    lane = lane_of((SLOTS, LANES))
    owner = lane_of((1, LANES)) // BLK
    for s in range(SLOTS):
        row = jnp.zeros((1, LANES), f32)
        live = jnp.zeros((1, LANES), f32)
        for b in range(LANES // BLK):
            number = ids_s[s, b]
            value = strain_s[variant_s[jnp.minimum(number, grains - 1)]]
            row = jnp.where(owner == b, jnp.where(number < grains, value, 0.0), row)
            live = jnp.where(owner == b, jnp.where(number < grains, 1.0, 0.0), live)
        st[pl.ds(s, 1), :] = row
        act[pl.ds(s, 1), :] = live
    tail = pl.ds(FACE + BLK, SLOTS)
    ztail = pl.ds(FACE // 2 + 8, SLOTS)
    beside = [xm[tail, :], xp[tail, :], ym[tail, :], yp[tail, :]]
    beside.append(jnp.where(lane < BLK, roll(zl[ztail, :], BLK), roll(own, BLK)))
    beside.append(jnp.where(lane >= LANES - BLK, roll(zr[ztail, :], -BLK), roll(own, -BLK)))
    for direction in range(6):
        for s in range(SLOTS):
            mine = own[s : s + 1, :]
            mk[direction, s] = jnp.where(
                (mine == beside[direction]) & (mine < float(grains)), 1.0, 0.0
            )

    lane2 = lane_of((BLK, LANES))
    row2 = lax.broadcasted_iota(jnp.int32, (BLK, LANES), 0)
    urow = pl.ds(FACE, BLK)
    wrow = pl.ds(FACE // 2, 8)
    wl = zl[wrow, :]
    wr = zr[wrow, :]
    for x in range(BLK):
        up = xp[urow, :] if x == BLK - 1 else dp[pl.ds((x + 1) * BLK, BLK), :]
        down = xm[urow, :] if x == 0 else dp[pl.ds((x - 1) * BLK, BLK), :]
        v = dp[pl.ds(PLANE + x * BLK, BLK), :]
        vp = jnp.where(row2 == BLK - 1, yp[pl.ds(FACE + x, 1), :], pltpu.roll(v, BLK - 1, axis=0))
        vm = jnp.where(row2 == 0, ym[pl.ds(FACE + x, 1), :], pltpu.roll(v, 1, axis=0))
        w = dp[pl.ds(2 * PLANE + x * BLK, BLK), :]
        right = jnp.concatenate([roll(wr, LANES - 1 - x), roll(wr, LANES - 1 - BLK - x)], axis=0)
        left = jnp.concatenate([roll(wl, BLK - x), roll(wl, 2 * BLK - x)], axis=0)
        wp = jnp.where(lane2 == LANES - 1, right, roll(w, -1))
        wm = jnp.where(lane2 == 0, left, roll(w, 1))
        dil[x] = 0.5 * ((up - down) + (vp - vm) + (wp - wm))

    def load(s, x):
        rows = pl.ds(pl.multiple_of(s * PLANE + x * BLK, BLK), BLK)
        return ph[rows, :] * act[pl.ds(s, 1), :]

    faces = (
        lambda t: xm[pl.ds(t * BLK, BLK), :],
        lambda t: xp[pl.ds(t * BLK, BLK), :],
        lambda t: ym[pl.ds(t * BLK, BLK), :],
        lambda t: yp[pl.ds(t * BLK, BLK), :],
        lambda t: zl[pl.ds(t * 8, 8), :],
        lambda t: zr[pl.ds(t * 8, 8), :],
    )
    update_phases(load, pp, mk, st, faces, pk, dil, out, e_out, pk_out, mv)
    for s in range(SLOTS):
        low, high = pl.ds(0, 8), pl.ds(8, 8)
        zphase[pl.ds(s * 8, 8), :] = fold_faces(
            pk_out[0, s, low, :], pk_out[0, s, high, :], pk_out[1, s, low, :], pk_out[1, s, high, :]
        )
    halo = REACH
    fields = field_rows(dp, e_out)
    x_sides(fields, halo, xlo, xhi)
    for s in range(SLOTS):
        rows = pl.ds(4 * halo * BLK + s * BLK, BLK)
        xlo[rows, :] = out[pl.ds(s * PLANE, BLK), :]
        xhi[rows, :] = out[pl.ds(s * PLANE + PLANE - BLK, BLK), :]


def field_rows(dp, e):
    def rows(f, x, y, n):
        if f < 3:
            return dp[pl.ds(f * PLANE + x * BLK + y, n), :]
        return e[pl.ds(x * BLK + y, n), :]

    return rows


def x_sides(fields, halo, xlo, xhi):
    for f in range(4):
        for k in range(halo):
            rows = pl.ds((f * halo + k) * BLK, BLK)
            xlo[rows, :] = fields(f, k, 0, BLK)
            xhi[rows, :] = fields(f, BLK - halo + k, 0, BLK)


def extended_rows(fields, xm, xp, halo):
    def rows(f, i, y, n):
        if i < halo:
            return xm[pl.ds((f * halo + i) * BLK + y, n), :]
        if i >= halo + BLK:
            return xp[pl.ds((f * halo + i - halo - BLK) * BLK + y, n), :]
        return fields(f, i - halo, y, n)

    return rows


def y_kernel(halo, with_phases, *refs):
    if with_phases:
        dp, e, xm, xp, ph, ylo, yhi = refs
    else:
        dp, e, xm, xp, ylo, yhi = refs
    rows = extended_rows(field_rows(dp, e), xm, xp, halo)
    count = BLK + 2 * halo
    for f in range(4):
        for i in range(count):
            place = pl.ds((f * count + i) * halo, halo)
            ylo[place, :] = rows(f, i, 0, halo)
            yhi[place, :] = rows(f, i, BLK - halo, halo)
    if with_phases:
        for s in range(SLOTS):
            place = pl.ds(4 * count * halo + s * BLK, BLK)
            ylo[place, :] = ph[pl.ds(s * PLANE, BLK, stride=BLK), :]
            yhi[place, :] = ph[pl.ds(s * PLANE + BLK - 1, BLK, stride=BLK), :]


def pack_width(halo):
    return 8 if halo > 2 else 4


def z_kernel(halo, with_phases, *refs):
    if with_phases:
        dp, e, xm, xp, ym, yp, zphase, zm, field = refs
    else:
        dp, e, xm, xp, ym, yp, zm, field = refs
    rows = extended_rows(field_rows(dp, e), xm, xp, halo)
    count = BLK + 2 * halo
    skip = REACH - halo
    width = pack_width(halo)
    per = LANES // width
    groups = -(-count // per)
    lane = lane_of((TALL, LANES))
    spot = lane // width
    for f in range(4):
        packs = [jnp.zeros((TALL, LANES), f32) for _ in range(groups)]
        for i in range(count):
            field[f, i + skip, pl.ds(OWN_Y, BLK), :] = rows(f, i, 0, BLK)
            side = pl.ds((f * count + i) * halo, halo)
            field[f, i + skip, pl.ds(OWN_Y - halo, halo), :] = ym[side, :]
            field[f, i + skip, pl.ds(OWN_Y + BLK, halo), :] = yp[side, :]
            value = field[f, i + skip, pl.ds(TOP, TALL), :]
            g, k = i // per, i % per
            packs[g] = jnp.where(spot == k, roll(value, width * k + width // 2), packs[g])
        for g in range(groups):
            zm[pl.ds((f * groups + g) * TALL, TALL), :] = packs[g]
    if with_phases:
        zm[pl.ds(4 * groups * TALL, FACE // 2), :] = zphase[...]


def shift_z(main, wing, sign):
    edge = lane_of(main.shape) == (0 if sign > 0 else LANES - 1)
    return roll(jnp.where(edge, wing, main), -sign)


def sweep(src, e, write, first, stop, windows, outer):
    turn = 0.5 * (lame_first + shear) * 0.5
    bulk = 0.5 * bulk_trace
    own = shear + (lame_first + shear)
    keep = 1.0 - relax_step * (6.0 * shear + 2.0 * (lame_first + shear))

    def layer(i, _):
        for r in windows:
            here, ups, downs = [], [], []
            for tile in range(2):
                u, v, w = [src(tile, k, i, r) for k in range(3)]
                gx = turn * (src(tile, 2, i + 1, r) - src(tile, 2, i - 1, r))
                gy = turn * (src(tile, 2, i, r + 1) - src(tile, 2, i, r - 1))
                gz = turn * (
                    (src(tile, 0, i + 1, r) - src(tile, 0, i - 1, r))
                    + (src(tile, 1, i, r + 1) - src(tile, 1, i, r - 1))
                ) - bulk * e(tile, i, r)
                wide = own * w
                here.append((u, v, w))
                ups.append((u + gx, v + gy, wide + gz))
                downs.append((u - gx, v - gy, wide - gz))
            for tile in range(2):
                for k in range(3):
                    if tile and k not in outer:
                        continue
                    lane_part = shift_z(ups[tile][k], ups[1 - tile][k], 1) + shift_z(
                        downs[tile][k], downs[1 - tile][k], -1
                    )
                    x_part = src(tile, k, i + 1, r) + src(tile, k, i - 1, r)
                    y_part = src(tile, k, i, r + 1) + src(tile, k, i, r - 1)
                    if k < 2:
                        o = 1 - k
                        cross = (src(tile, o, i + 1, r + 1) - src(tile, o, i + 1, r - 1)) - (
                            src(tile, o, i - 1, r + 1) - src(tile, o, i - 1, r - 1)
                        )
                        if k == 0:
                            slope = e(tile, i + 1, r) - e(tile, i - 1, r)
                            near = own * x_part + y_part
                        else:
                            slope = e(tile, i, r + 1) - e(tile, i, r - 1)
                            near = own * y_part + x_part
                        change = near + lane_part + (turn * cross - bulk * slope)
                    else:
                        change = (x_part + y_part) + lane_part
                    write(tile, k, i, r, keep * here[tile][k] + relax_step * change)
        return 0

    lax.fori_loop(first, stop, layer, 0, unroll=True)


def relax(halo, field, zl, zr, wing, mid, write, outer):
    count = BLK + 2 * halo
    skip = REACH - halo
    width = pack_width(halo)
    per = LANES // width
    groups = -(-count // per)
    lane = lane_of((TALL, LANES))
    right = lane % width >= width // 2
    for f in range(4):
        packs = []
        for g in range(groups):
            rows = pl.ds((f * groups + g) * TALL, TALL)
            packs.append(jnp.where(right, zr[rows, :], zl[rows, :]))
        for i in range(count):
            g, k = i // per, i % per
            wing[f, i + skip, pl.ds(TOP, TALL), :] = roll(packs[g], -width * k - width // 2)
    first, stop = skip + 1, skip + count - 1
    low, high = OWN_Y - halo + 1, OWN_Y + BLK + halo - 1

    def spans(low, high):
        return sorted({min(r, high - 8) for r in range(low, high, 8)})

    fields = (field, wing)

    def load(tile, k, i, r):
        return fields[tile][k, i, pl.ds(r, 8), :]

    def load_mid(tile, k, i, r):
        return mid[tile, k, i, pl.ds(r, 8), :]

    def load_e(tile, i, r):
        return fields[tile][3, i, pl.ds(r, 8), :]

    def write_mid(tile, k, i, r, value):
        mid[tile, k, i, pl.ds(r, 8), :] = value

    sweep(load, load_e, write_mid, first, stop, spans(low, high), (0, 1, 2))
    sweep(load_mid, load_e, write, first + 1, stop - 1, spans(low + 1, high - 1), outer)


def second_kernel(
    field, zl, zr, ph, pk, mk, st, xm, xp, ym, yp,
    out, e_out, moved, xlo, xhi, wing, mid, end, pp, dil, mv,
):
    halo = REACH

    def write(tile, k, i, r, value):
        end[k + tile, i, pl.ds(r, 8), :] = value

    relax(halo, field, zl, zr, wing, mid, write, (2,))

    def strain_rate(x, _):
        i = x + REACH
        for half in range(2):
            r = OWN_Y + 8 * half
            rows = pl.ds(r, 8)
            w, side = end[2, i, rows, :], end[3, i, rows, :]
            dil[x, pl.ds(8 * half, 8), :] = 0.5 * (
                (end[0, i + 1, rows, :] - end[0, i - 1, rows, :])
                + (end[1, i, pl.ds(r + 1, 8), :] - end[1, i, pl.ds(r - 1, 8), :])
                + (shift_z(w, side, 1) - shift_z(w, side, -1))
            )
            for k in range(3):
                moved[pl.ds(pl.multiple_of(k * PLANE + x * BLK + 8 * half, 8), 8), :] = end[
                    k, i, rows, :
                ]
        return 0

    lax.fori_loop(0, BLK, strain_rate, 0)
    count = BLK + 2 * halo
    xbase = 4 * halo * BLK
    ybase = 4 * count * halo
    zbase = 4 * (-(-count // (LANES // pack_width(halo)))) * TALL

    def load(s, x):
        return ph[pl.ds(pl.multiple_of(s * PLANE + x * BLK, BLK), BLK), :]

    faces = (
        lambda t: xm[pl.ds(xbase + t * BLK, BLK), :],
        lambda t: xp[pl.ds(xbase + t * BLK, BLK), :],
        lambda t: ym[pl.ds(ybase + t * BLK, BLK), :],
        lambda t: yp[pl.ds(ybase + t * BLK, BLK), :],
        lambda t: zl[pl.ds(zbase + t * 8, 8), :],
        lambda t: zr[pl.ds(zbase + t * 8, 8), :],
    )
    update_phases(load, pp, mk, st, faces, pk, dil, out, e_out, None, mv)
    x_sides(field_rows(moved, e_out), SWEEPS, xlo, xhi)


def last_kernel(field, zl, zr, moved, wing, mid):
    def write(tile, k, i, r, value):
        place = k * PLANE + (i - REACH) * BLK + (r - OWN_Y)
        moved[pl.ds(pl.multiple_of(place, 8), 8), :] = value

    relax(SWEEPS, field, zl, zr, wing, mid, write, ())


def rows_of(n):
    return jax.ShapeDtypeStruct((n, LANES), f32)


def call(kernel, outs, args, scratch=(), scalars=0, name=None):
    vmem = pl.BlockSpec(memory_space=pltpu.VMEM)
    smem = pl.BlockSpec(memory_space=pltpu.SMEM)
    return pl.pallas_call(
        kernel,
        out_shape=outs,
        in_specs=[smem] * scalars + [vmem] * (len(args) - scalars),
        out_specs=jax.tree.map(lambda _: vmem, outs),
        scratch_shapes=[pltpu.VMEM(shape, f32) for shape in scratch],
        name=name,
        compiler_params=pltpu.CompilerParams(vmem_limit_bytes=40 * 2**20),
    )(*args)


def swap(low, high, axis):
    n = lax.axis_size(axis)
    below = lax.ppermute(high, axis, [(i, (i + 1) % n) for i in range(n)])
    if low is high and n == 2:
        return below, below
    above = lax.ppermute(low, axis, [((i + 1) % n, i) for i in range(n)])
    return below, above


def local(phase, displacement, slot_ids, grain_variant, variant_strain):
    ph = phase.reshape(-1, LANES)
    dp = displacement.reshape(-1, LANES)
    ids = slot_ids.reshape(SLOTS, -1)
    side = rows_of(FACE + BLK + SLOTS)
    packed = jax.ShapeDtypeStruct((2, SLOTS, BLK, LANES), f32)
    padded = (SLOTS, BLK + 2, 32, LANES)
    square = (BLK, BLK, LANES)
    turned = (2, SLOTS, BLK, LANES)
    wide = (4, WIDE, PITCH, LANES)
    double = (2, 3, WIDE, PITCH, LANES)

    xlo, xhi, ylo, yhi, zm, pk = call(
        start_kernel,
        (side, side, side, side, rows_of(FACE // 2 + 8 + SLOTS), packed),
        (ph, dp, ids),
        name="start",
    )
    xm, xp = swap(xlo, xhi, "gx")
    ym, yp = swap(ylo, yhi, "gy")
    zl, zr = swap(zm, zm, "gz")

    halo = REACH
    count = BLK + 2 * halo
    groups = -(-count // (LANES // pack_width(halo)))
    xside = rows_of(4 * halo * BLK + FACE)
    phases, eigen, pk, zphase, xlo, xhi, mk, st = call(
        first_kernel,
        (
            rows_of(SLOTS * PLANE),
            rows_of(PLANE),
            packed,
            rows_of(FACE // 2),
            xside,
            xside,
            jax.ShapeDtypeStruct((6, SLOTS, SLOTS, LANES), f32),
            rows_of(SLOTS),
        ),
        (ids, grain_variant, variant_strain, ids, ph, dp, pk, xm, xp, ym, yp, zl, zr),
        scratch=(padded, square, turned, (SLOTS, LANES)),
        scalars=3,
        name="first",
    )
    xm, xp = swap(xlo, xhi, "gx")
    yside = rows_of(4 * count * halo + FACE)
    ylo, yhi = call(
        functools.partial(y_kernel, halo, True),
        (yside, yside),
        (dp, eigen, xm, xp, phases),
        name="rows_a",
    )
    ym, yp = swap(ylo, yhi, "gy")
    field_shape = jax.ShapeDtypeStruct(wide, f32)
    zm, field = call(
        functools.partial(z_kernel, halo, True),
        (rows_of(4 * groups * TALL + FACE // 2), field_shape),
        (dp, eigen, xm, xp, ym, yp, zphase),
        name="lanes_a",
    )
    zl, zr = swap(zm, zm, "gz")
    halo = SWEEPS
    count = BLK + 2 * halo
    groups = -(-count // (LANES // pack_width(halo)))
    xside = rows_of(4 * halo * BLK)
    phases, eigen, moved, xlo, xhi = call(
        second_kernel,
        (rows_of(SLOTS * PLANE), rows_of(PLANE), rows_of(3 * PLANE), xside, xside),
        (field, zl, zr, phases, pk, mk, st, xm, xp, ym, yp),
        scratch=(wide, double, wide, padded, square, turned),
        name="second",
    )
    xm, xp = swap(xlo, xhi, "gx")
    yside = rows_of(4 * count * halo)
    ylo, yhi = call(
        functools.partial(y_kernel, halo, False),
        (yside, yside),
        (moved, eigen, xm, xp),
        name="rows_b",
    )
    ym, yp = swap(ylo, yhi, "gy")
    zm, field = call(
        functools.partial(z_kernel, halo, False),
        (rows_of(4 * groups * TALL), field_shape),
        (moved, eigen, xm, xp, ym, yp),
        name="lanes_b",
    )
    zl, zr = swap(zm, zm, "gz")
    moved = call(
        last_kernel,
        rows_of(3 * PLANE),
        (field, zl, zr),
        scratch=(wide, double),
        name="last",
    )
    return phases.reshape(phase.shape), moved.reshape(displacement.shape)


def solution(mesh):
    spec = P(None, "gx", "gy", "gz")
    return jax.shard_map(
        local,
        mesh=mesh,
        in_specs=(spec, spec, spec, P(), P()),
        out_specs=(spec, spec),
        check_vma=False,
    )
```

```python
import dataclasses

import jax
import jax.numpy as jnp
from jax import lax
from jax.experimental import pallas as pl
from jax.experimental.pallas import tpu as pltpu
from jax.sharding import PartitionSpec as P


SLOTS = 8
BLK = 16
SWEEPS = 2

well_linear = 1.0
well_cubic = 1.0
cross_term = 1.5
gradient_energy = 2.0
time_step = 0.04
shear = 1.0
lame_first = 1.0
relax_step = 0.06
bulk_trace = 3.0 * lame_first + 2.0 * shear

LANES = 128
PLANE = BLK * BLK
REACH = 2 * SWEEPS
WIDE = BLK + 2 * REACH
GROUP = 2 * REACH
FACE = SLOTS * BLK
SIDE = FACE + BLK + SLOTS
ZD = FACE // 2

f32 = jnp.float32


def lane_of(shape):
    return lax.broadcasted_iota(jnp.int32, shape, len(shape) - 1)


def roll(value, shift):
    if isinstance(shift, int):
        shift = shift % LANES
        if shift == 0:
            return value
    else:
        shift = lax.rem(shift + 2 * LANES, LANES)
    return pltpu.roll(value, shift, axis=value.ndim - 1)


def grow(ids):
    lane = lane_of((SLOTS, LANES)) // BLK
    out = jnp.zeros((SLOTS, LANES), f32)
    values = ids.astype(f32)
    for b in range(LANES // BLK):
        out = jnp.where(lane == b, jnp.broadcast_to(values[:, b : b + 1], (SLOTS, LANES)), out)
    return out


def fold_faces(first0, first1, last0, last1):
    lane = lane_of(first0.shape)
    return jnp.where(
        lane < BLK,
        first0,
        jnp.where(
            lane < 2 * BLK,
            roll(first1, BLK),
            jnp.where(lane < LANES - BLK, roll(last1, -BLK), last0),
        ),
    )


def faces_kernel(ph, xlo, xhi, ylo, yhi, zm, pk):
    for s in range(SLOTS):
        rows = pl.ds(s * BLK, BLK)
        xlo[rows, :] = ph[pl.ds(s * PLANE, BLK), :]
        xhi[rows, :] = ph[pl.ds(s * PLANE + PLANE - BLK, BLK), :]
        ylo[rows, :] = ph[pl.ds(s * PLANE, BLK, stride=BLK), :]
        yhi[rows, :] = ph[pl.ds(s * PLANE + BLK - 1, BLK, stride=BLK), :]
    spot = lane_of((8, LANES)) % BLK
    for f in range(SLOTS):
        packs = []
        for half in range(2):
            first = jnp.zeros((8, LANES), f32)
            last = jnp.zeros((8, LANES), f32)
            for x in range(BLK):
                value = ph[pl.ds(f * PLANE + x * BLK + 8 * half, 8), :]
                first = jnp.where(spot == x, roll(value, x), first)
                last = jnp.where(spot == x, roll(value, x - BLK + 1), last)
            packs.append((first, last))
            pk[0, f, pl.ds(8 * half, 8), :] = first
            pk[1, f, pl.ds(8 * half, 8), :] = last
        zm[pl.ds(f * 8, 8), :] = fold_faces(packs[0][0], packs[1][0], packs[0][1], packs[1][1])


def start_kernel(dp, ids, *refs):
    for source, ref in zip(refs[:5], refs[5:]):
        rows = pl.ds(0, source.shape[0])
        ref[rows, :] = source[...]
    xlo, xhi, ylo, yhi, zm = refs[5:]
    numbers = grow(ids[...])
    rows = pl.ds(FACE, BLK)
    xlo[rows, :] = dp[pl.ds(0, BLK), :]
    xhi[rows, :] = dp[pl.ds(PLANE - BLK, BLK), :]
    ylo[rows, :] = dp[pl.ds(PLANE, BLK, stride=BLK), :]
    yhi[rows, :] = dp[pl.ds(PLANE + BLK - 1, BLK, stride=BLK), :]
    for ref in (xlo, xhi, ylo, yhi):
        ref[pl.ds(FACE + BLK, SLOTS), :] = numbers
    zm[pl.ds(ZD + 3 * BLK, SLOTS), :] = numbers
    for f in range(3):
        zm[pl.ds(ZD + f * BLK, BLK), :] = pack_ends(
            lambda x: dp[pl.ds(f * PLANE + x * BLK, BLK), :], BLK
        )


def pack_ends(layer, rows):
    spot = lane_of((rows, LANES)) // GROUP
    out = jnp.zeros((rows, LANES), f32)
    for x in range(BLK):
        out = jnp.where(spot == x, roll(layer(x), GROUP * x + REACH), out)
    return out


def unpack_ends(packed, x):
    return roll(packed, -(GROUP * x + REACH))


def join_ends(left, right):
    return jnp.where(lane_of(left.shape) % GROUP >= REACH, right, left)


def update_phases(load, pp, mk, st, faces, pk, dil, out, e_out, pk_out, mv):
    xm, xp, ym, yp, zl, zr = faces
    lane = lane_of((8, LANES))
    spot = lane % BLK

    def fill(x, _):
        for s in range(SLOTS):
            pp[s, x + 1, pl.ds(8, BLK), :] = load(s, x)
        return 0

    lax.fori_loop(0, BLK, fill, 0)

    def match(direction, s, layers):
        total = None
        for t in range(SLOTS):
            term = mk[direction, s, pl.ds(t, 1), :] * layers[t]
            total = term if total is None else total + term
        return total

    for direction, face, place in ((0, xm, 0), (1, xp, BLK + 1)):
        layers = [face(t) for t in range(SLOTS)]
        for s in range(SLOTS):
            pp[s, place, pl.ds(8, BLK), :] = match(direction, s, layers)
    for direction, face, place in ((2, ym, 7), (3, yp, 8 + BLK)):
        layers = [face(t) for t in range(SLOTS)]
        for s in range(SLOTS):
            moved = match(direction, s, layers)
            for x in range(BLK):
                pp[s, x + 1, pl.ds(place, 1), :] = moved[x : x + 1, :]
    for half in range(2):
        rows = pl.ds(8 * half, 8)
        before = [
            jnp.where(lane < BLK, roll(zl(t), BLK * (1 + half)), roll(pk[1, t, rows, :], BLK))
            for t in range(SLOTS)
        ]
        for s in range(SLOTS):
            mv[0, s, rows, :] = match(4, s, before)
        after = [
            jnp.where(
                lane >= LANES - BLK, roll(zr(t), -BLK * (1 + half)), roll(pk[0, t, rows, :], -BLK)
            )
            for t in range(SLOTS)
        ]
        for s in range(SLOTS):
            mv[1, s, rows, :] = match(5, s, after)

    if pk_out is not None:
        pk_out[...] = jnp.zeros(pk_out.shape, f32)

    def layer(x, _):
        for half in range(2):
            r0 = 8 + 8 * half
            rows = pl.ds(8 * half, 8)
            values = [pp[s, x + 1, pl.ds(r0, 8), :] for s in range(SLOTS)]
            total = None
            eigen = None
            for s in range(SLOTS):
                square = values[s] * values[s]
                part = square * st[pl.ds(s, 1), :]
                total = square if total is None else total + square
                eigen = part if eigen is None else eigen + part
            trace = bulk_trace * (dil[x, rows, :] - 3.0 * eigen)
            base = (1.0 + time_step * well_linear - 6.0 * time_step * gradient_energy) - (
                2.0 * cross_term * time_step
            ) * total
            pull = (2.0 * time_step) * trace
            fresh = None
            for s in range(SLOTS):
                p = values[s]
                after = jnp.where(
                    spot == BLK - 1, roll(mv[1, s, rows, :], BLK - 1 - x), roll(p, -1)
                )
                before = jnp.where(spot == 0, roll(mv[0, s, rows, :], -x), roll(p, 1))
                near = (
                    (pp[s, x, pl.ds(r0, 8), :] + pp[s, x + 2, pl.ds(r0, 8), :])
                    + (pp[s, x + 1, pl.ds(r0 - 1, 8), :] + pp[s, x + 1, pl.ds(r0 + 1, 8), :])
                    + (after + before)
                )
                rate = (
                    base
                    + (time_step * (2.0 * cross_term - well_cubic)) * (p * p)
                    + pull * st[pl.ds(s, 1), :]
                )
                new = p * rate + (time_step * gradient_energy) * near
                out[pl.ds(pl.multiple_of(s * PLANE + x * BLK + 8 * half, 8), 8), :] = new
                part = new * new * st[pl.ds(s, 1), :]
                fresh = part if fresh is None else fresh + part
                if pk_out is not None:
                    pk_out[0, s, rows, :] = jnp.where(
                        spot == x, roll(new, x), pk_out[0, s, rows, :]
                    )
                    pk_out[1, s, rows, :] = jnp.where(
                        spot == x, roll(new, x - BLK + 1), pk_out[1, s, rows, :]
                    )
            e_out[pl.ds(pl.multiple_of(x * BLK + 8 * half, 8), 8), :] = fresh
        return 0

    lax.fori_loop(0, BLK, layer, 0)


def first_kernel(
    ids_s, variant_s, strain_s, ids, ph, dp, pk, xm, xp, ym, yp, zl, zr,
    out, e_out, pk_out, zm, ylo, yhi, mk, st, pp, dil, mv, act,
):
    grains = variant_s.shape[0]
    own = grow(ids[...])
    lane = lane_of((SLOTS, LANES))
    owner = lane_of((1, LANES)) // BLK
    for s in range(SLOTS):
        row = jnp.zeros((1, LANES), f32)
        live = jnp.zeros((1, LANES), f32)
        for b in range(LANES // BLK):
            number = ids_s[s, b]
            value = strain_s[variant_s[jnp.minimum(number, grains - 1)]]
            row = jnp.where(owner == b, jnp.where(number < grains, value, 0.0), row)
            live = jnp.where(owner == b, jnp.where(number < grains, 1.0, 0.0), live)
        st[pl.ds(s, 1), :] = row
        act[pl.ds(s, 1), :] = live
    tail = pl.ds(FACE + BLK, SLOTS)
    ztail = pl.ds(ZD + 3 * BLK, SLOTS)
    beside = [xm[tail, :], xp[tail, :], ym[tail, :], yp[tail, :]]
    beside.append(jnp.where(lane < BLK, roll(zl[ztail, :], BLK), roll(own, BLK)))
    beside.append(jnp.where(lane >= LANES - BLK, roll(zr[ztail, :], -BLK), roll(own, -BLK)))
    for direction in range(6):
        for s in range(SLOTS):
            mine = own[s : s + 1, :]
            mk[direction, s] = jnp.where(
                (mine == beside[direction]) & (mine < float(grains)), 1.0, 0.0
            )

    lane2 = lane_of((BLK, LANES))
    row2 = lax.broadcasted_iota(jnp.int32, (BLK, LANES), 0)
    urow = pl.ds(FACE, BLK)
    wrow = pl.ds(ZD + 2 * BLK, BLK)
    ends = join_ends(zl[wrow, :], zr[wrow, :])
    for x in range(BLK):
        up = xp[urow, :] if x == BLK - 1 else dp[pl.ds((x + 1) * BLK, BLK), :]
        down = xm[urow, :] if x == 0 else dp[pl.ds((x - 1) * BLK, BLK), :]
        v = dp[pl.ds(PLANE + x * BLK, BLK), :]
        vp = jnp.where(row2 == BLK - 1, yp[pl.ds(FACE + x, 1), :], pltpu.roll(v, BLK - 1, axis=0))
        vm = jnp.where(row2 == 0, ym[pl.ds(FACE + x, 1), :], pltpu.roll(v, 1, axis=0))
        w = dp[pl.ds(2 * PLANE + x * BLK, BLK), :]
        edge = unpack_ends(ends, x)
        dil[x] = 0.5 * ((up - down) + (vp - vm) + (shift_z(w, edge, 1) - shift_z(w, edge, -1)))

    def load(s, x):
        rows = pl.ds(pl.multiple_of(s * PLANE + x * BLK, BLK), BLK)
        return ph[rows, :] * act[pl.ds(s, 1), :]

    faces = (
        lambda t: xm[pl.ds(t * BLK, BLK), :],
        lambda t: xp[pl.ds(t * BLK, BLK), :],
        lambda t: ym[pl.ds(t * BLK, BLK), :],
        lambda t: yp[pl.ds(t * BLK, BLK), :],
        lambda t: zl[pl.ds(t * 8, 8), :],
        lambda t: zr[pl.ds(t * 8, 8), :],
    )
    update_phases(load, pp, mk, st, faces, pk, dil, out, e_out, pk_out, mv)
    for s in range(SLOTS):
        low, high = pl.ds(0, 8), pl.ds(8, 8)
        zm[pl.ds(s * 8, 8), :] = fold_faces(
            pk_out[0, s, low, :], pk_out[0, s, high, :], pk_out[1, s, low, :], pk_out[1, s, high, :]
        )
        rows = pl.ds(s * BLK, BLK)
        ylo[rows, :] = out[pl.ds(s * PLANE, BLK, stride=BLK), :]
        yhi[rows, :] = out[pl.ds(s * PLANE + BLK - 1, BLK, stride=BLK), :]
    zm[pl.ds(ZD, BLK), :] = pack_ends(lambda x: e_out[pl.ds(x * BLK, BLK), :], BLK)
    y_sides(e_out, REACH, FACE, ylo, yhi)


def y_sides(e, halo, base, ylo, yhi):
    for x in range(BLK):
        rows = pl.ds(base + x * halo, halo)
        ylo[rows, :] = e[pl.ds(x * BLK, halo), :]
        yhi[rows, :] = e[pl.ds(x * BLK + BLK - halo, halo), :]


def move_rows_kernel(dp, zl, zr, ylo, yhi, ends):
    for f in range(3):
        rows = pl.ds(ZD + f * BLK, BLK)
        ends[f] = join_ends(zl[rows, :], zr[rows, :])
        for x in range(BLK):
            place = pl.ds((f * BLK + x) * REACH, REACH)
            start = f * PLANE + x * BLK
            ylo[place, :] = dp[pl.ds(start, REACH), :]
            yhi[place, :] = dp[pl.ds(start + BLK - REACH, REACH), :]
        place = pl.ds(3 * BLK * REACH + f * REACH, REACH)
        ylo[place, :] = ends[f, pl.ds(0, REACH), :]
        yhi[place, :] = ends[f, pl.ds(BLK - REACH, REACH), :]


def move_layers_kernel(dp, ym, yp, ends, xlo, xhi, tall):
    inner = pl.ds(REACH, BLK)
    for f in range(3):
        side = pl.ds(3 * BLK * REACH + f * REACH, REACH)
        tall[f, pl.ds(0, REACH), :] = ym[side, :]
        tall[f, inner, :] = ends[f]
        tall[f, pl.ds(REACH + BLK, REACH), :] = yp[side, :]
        for ref, first in ((xlo, 0), (xhi, BLK - REACH)):
            for k in range(REACH):
                x = first + k
                base = (f * REACH + k) * WIDE
                side = pl.ds((f * BLK + x) * REACH, REACH)
                ref[pl.ds(base, REACH), :] = ym[side, :]
                ref[pl.ds(base + REACH, BLK), :] = dp[pl.ds(f * PLANE + x * BLK, BLK), :]
                ref[pl.ds(base + REACH + BLK, REACH), :] = yp[side, :]
            ref[pl.ds((3 * REACH + f) * WIDE, WIDE), :] = tall[f]


def spread_kernel(dp, ym, yp, tall, xm, xp, main, wing):
    for f in range(3):
        for x in range(BLK):
            side = pl.ds((f * BLK + x) * REACH, REACH)
            i = x + REACH
            main[f, i, pl.ds(0, REACH), :] = ym[side, :]
            main[f, i, pl.ds(REACH, BLK), :] = dp[pl.ds(f * PLANE + x * BLK, BLK), :]
            main[f, i, pl.ds(REACH + BLK, REACH), :] = yp[side, :]
            wing[f, i] = unpack_ends(tall[f], x)
        ends = pl.ds((3 * REACH + f) * WIDE, WIDE)
        for k in range(REACH):
            rows = pl.ds((f * REACH + k) * WIDE, WIDE)
            main[f, k] = xm[rows, :]
            main[f, REACH + BLK + k] = xp[rows, :]
            wing[f, k] = unpack_ends(xm[ends, :], BLK - REACH + k)
            wing[f, REACH + BLK + k] = unpack_ends(xp[ends, :], k)


def strain_rows_kernel(zl, zr, ylo, yhi, ends):
    rows = pl.ds(ZD, BLK)
    joined = join_ends(zl[rows, :], zr[rows, :])
    ends[...] = joined
    ylo[...] = joined[:8, :]
    yhi[...] = joined[BLK - 8 :, :]


def strain_layers_kernel(e, ph, ym, yp, em, ep, ends, xlo, xhi, tall):
    tall[pl.ds(0, REACH), :] = em[pl.ds(8 - REACH, REACH), :]
    tall[pl.ds(REACH, BLK), :] = ends[...]
    tall[pl.ds(REACH + BLK, REACH), :] = ep[pl.ds(0, REACH), :]
    for ref, first in ((xlo, 0), (xhi, BLK - REACH)):
        for s in range(SLOTS):
            x = 0 if first == 0 else BLK - 1
            ref[pl.ds(s * BLK, BLK), :] = ph[pl.ds(s * PLANE + x * BLK, BLK), :]
        for k in range(REACH):
            x = first + k
            base = FACE + k * WIDE
            side = pl.ds(FACE + x * REACH, REACH)
            ref[pl.ds(base, REACH), :] = ym[side, :]
            ref[pl.ds(base + REACH, BLK), :] = e[pl.ds(x * BLK, BLK), :]
            ref[pl.ds(base + REACH + BLK, REACH), :] = yp[side, :]
        ref[pl.ds(FACE + REACH * WIDE, WIDE), :] = tall[...]


def shift_z(main, wing, sign):
    edge = lane_of(main.shape) == (0 if sign > 0 else LANES - 1)
    return roll(jnp.where(edge, wing, main), -sign)


def sweep(src, e, write, first, stop, windows, outer):
    turn = 0.5 * (lame_first + shear) * 0.5
    bulk = 0.5 * bulk_trace
    own = shear + (lame_first + shear)
    keep = 1.0 - relax_step * (6.0 * shear + 2.0 * (lame_first + shear))

    def layer(i, _):
        for r in windows:
            here, ups, downs = [], [], []
            for tile in range(2):
                u, v, w = [src(tile, k, i, r) for k in range(3)]
                gx = turn * (src(tile, 2, i + 1, r) - src(tile, 2, i - 1, r))
                gy = turn * (src(tile, 2, i, r + 1) - src(tile, 2, i, r - 1))
                gz = turn * (
                    (src(tile, 0, i + 1, r) - src(tile, 0, i - 1, r))
                    + (src(tile, 1, i, r + 1) - src(tile, 1, i, r - 1))
                ) - bulk * e(tile, i, r)
                wide = own * w
                here.append((u, v, w))
                ups.append((u + gx, v + gy, wide + gz))
                downs.append((u - gx, v - gy, wide - gz))
            for tile in range(2):
                for k in range(3):
                    if tile and k not in outer:
                        continue
                    lane_part = shift_z(ups[tile][k], ups[1 - tile][k], 1) + shift_z(
                        downs[tile][k], downs[1 - tile][k], -1
                    )
                    x_part = src(tile, k, i + 1, r) + src(tile, k, i - 1, r)
                    y_part = src(tile, k, i, r + 1) + src(tile, k, i, r - 1)
                    if k < 2:
                        o = 1 - k
                        cross = (src(tile, o, i + 1, r + 1) - src(tile, o, i + 1, r - 1)) - (
                            src(tile, o, i - 1, r + 1) - src(tile, o, i - 1, r - 1)
                        )
                        if k == 0:
                            slope = e(tile, i + 1, r) - e(tile, i - 1, r)
                            near = own * x_part + y_part
                        else:
                            slope = e(tile, i, r + 1) - e(tile, i, r - 1)
                            near = own * y_part + x_part
                        change = near + lane_part + (turn * cross - bulk * slope)
                    else:
                        change = (x_part + y_part) + lane_part
                    write(tile, k, i, r, keep * here[tile][k] + relax_step * change)
        return 0

    lax.fori_loop(first, stop, layer, 0, unroll=True)


def relax(halo, main, wing, e, mid, write, outer):
    low, high = REACH - halo + 1, REACH + BLK + halo - 1

    def spans(low, high):
        return sorted({min(r, high - 8) for r in range(low, high, 8)})

    fields = (main, wing)

    def load(tile, k, i, r):
        return fields[tile][k, i, pl.ds(r, 8), :]

    def load_mid(tile, k, i, r):
        return mid[tile, k, i, pl.ds(r, 8), :]

    def load_e(tile, i, r):
        return e[tile, i, pl.ds(r, 8), :]

    def write_mid(tile, k, i, r, value):
        mid[tile, k, i, pl.ds(r, 8), :] = value

    sweep(load, load_e, write_mid, low, high, spans(low, high), (0, 1, 2))
    sweep(load_mid, load_e, write, low + 1, high - 1, spans(low + 1, high - 1), outer)


def second_kernel(
    main, wing, e_in, eym, eyp, tall, ph, pk, mk, st, xm, xp, ym, yp, zl, zr,
    out, e_out, moved, aside, xlo, xhi, ylo, yhi, zm, e, mid, pp, dil, mv,
):
    for x in range(BLK):
        i = x + REACH
        side = pl.ds(FACE + x * REACH, REACH)
        e[0, i, pl.ds(0, REACH), :] = ym[side, :]
        e[0, i, pl.ds(REACH, BLK), :] = e_in[pl.ds(x * BLK, BLK), :]
        e[0, i, pl.ds(REACH + BLK, REACH), :] = yp[side, :]
        e[1, i] = unpack_ends(tall[...], x)
    ends = pl.ds(FACE + REACH * WIDE, WIDE)
    for k in range(REACH):
        rows = pl.ds(FACE + k * WIDE, WIDE)
        e[0, k] = xm[rows, :]
        e[0, REACH + BLK + k] = xp[rows, :]
        e[1, k] = unpack_ends(xm[ends, :], BLK - REACH + k)
        e[1, REACH + BLK + k] = unpack_ends(xp[ends, :], k)

    results = (moved, aside)

    def write(tile, k, i, r, value):
        results[tile][k, i, pl.ds(r, 8), :] = value

    relax(REACH, main, wing, e, mid, write, (0, 1, 2))

    def strain_rate(x, _):
        i = x + REACH
        for half in range(2):
            r = REACH + 8 * half
            rows = pl.ds(r, 8)
            w, side = moved[2, i, rows, :], aside[2, i, rows, :]
            dil[x, pl.ds(8 * half, 8), :] = 0.5 * (
                (moved[0, i + 1, rows, :] - moved[0, i - 1, rows, :])
                + (moved[1, i, pl.ds(r + 1, 8), :] - moved[1, i, pl.ds(r - 1, 8), :])
                + (shift_z(w, side, 1) - shift_z(w, side, -1))
            )
        return 0

    lax.fori_loop(0, BLK, strain_rate, 0, unroll=True)

    def load(s, x):
        return ph[pl.ds(pl.multiple_of(s * PLANE + x * BLK, BLK), BLK), :]

    faces = (
        lambda t: xm[pl.ds(t * BLK, BLK), :],
        lambda t: xp[pl.ds(t * BLK, BLK), :],
        lambda t: ym[pl.ds(t * BLK, BLK), :],
        lambda t: yp[pl.ds(t * BLK, BLK), :],
        lambda t: zl[pl.ds(t * 8, 8), :],
        lambda t: zr[pl.ds(t * 8, 8), :],
    )
    update_phases(load, pp, mk, st, faces, pk, dil, out, e_out, None, mv)
    for k in range(SWEEPS):
        xlo[pl.ds(k * BLK, BLK), :] = e_out[pl.ds(k * BLK, BLK), :]
        xhi[pl.ds(k * BLK, BLK), :] = e_out[pl.ds((BLK - SWEEPS + k) * BLK, BLK), :]
    y_sides(e_out, SWEEPS, 0, ylo, yhi)
    zm[...] = pack_ends(lambda x: e_out[pl.ds(x * BLK, BLK), :], BLK)


def edges_kernel(ym, yp, zl, zr, xlo, xhi, zm):
    joined = join_ends(zl[...], zr[...])
    for ref, first in ((xlo, 0), (xhi, BLK - SWEEPS)):
        ref[pl.ds(0, BLK), :] = joined
        for k in range(SWEEPS):
            side = pl.ds((first + k) * SWEEPS, SWEEPS)
            ref[pl.ds(BLK + k * SWEEPS, SWEEPS), :] = ym[side, :]
            ref[pl.ds(BLK + (SWEEPS + k) * SWEEPS, SWEEPS), :] = yp[side, :]

    def rows(x):
        side = pl.ds(x * SWEEPS, SWEEPS)
        blank = jnp.zeros((8 - 2 * SWEEPS, LANES), f32)
        return jnp.concatenate([ym[side, :], yp[side, :], blank], axis=0)

    zm[...] = pack_ends(rows, 8)


def last_kernel(
    main, wing, e_in, xm, xp, ym, yp, zl, zr, xem, xep, zel, zer, out, e, mid
):
    n = SWEEPS
    before, after = REACH - n, REACH + BLK
    own = pl.ds(REACH, BLK)
    joined = join_ends(zl[...], zr[...])
    edges = join_ends(zel[...], zer[...])
    for x in range(BLK):
        i = x + REACH
        side = pl.ds(x * n, n)
        e[0, i, pl.ds(before, n), :] = ym[side, :]
        e[0, i, own, :] = e_in[pl.ds(x * BLK, BLK), :]
        e[0, i, pl.ds(after, n), :] = yp[side, :]
        e[1, i, own, :] = unpack_ends(joined, x)
        turned = unpack_ends(edges, x)
        e[1, i, pl.ds(before, n), :] = turned[:n, :]
        e[1, i, pl.ds(after, n), :] = turned[n : 2 * n, :]
    for k in range(n):
        rows = pl.ds(k * BLK, BLK)
        for flat, edge, i, x in ((xm, xem, before + k, BLK - n + k), (xp, xep, after + k, k)):
            e[0, i, own, :] = flat[rows, :]
            e[0, i, pl.ds(before, n), :] = edge[pl.ds(BLK + k * n, n), :]
            e[0, i, pl.ds(after, n), :] = edge[pl.ds(BLK + (n + k) * n, n), :]
            e[1, i, own, :] = unpack_ends(edge[pl.ds(0, BLK), :], x)

    def write(tile, k, i, r, value):
        place = k * PLANE + (i - REACH) * BLK + (r - REACH)
        out[pl.ds(place if isinstance(place, int) else pl.multiple_of(place, 8), 8), :] = value

    relax(n, main, wing, e, mid, write, ())


def rows_of(n):
    return jax.ShapeDtypeStruct((n, LANES), f32)


@dataclasses.dataclass(frozen=True)
class Sides:
    axis: str
    near: object
    far: object


def both(axis, rows):
    return Sides(axis, rows_of(rows), rows_of(rows))


def call(kernel, outs, args, scratch=(), scalars=0):
    vmem = pl.BlockSpec(memory_space=pltpu.VMEM)
    smem = pl.BlockSpec(memory_space=pltpu.SMEM)
    kinds = [*args, *outs]
    flat_in = [part for a in args for part in ((a.near, a.far) if isinstance(a, Sides) else (a,))]
    flat_out = [part for a in outs for part in ((a.near, a.far) if isinstance(a, Sides) else (a,))]
    pairs = [(2,) + a.near.shape for a in kinds if isinstance(a, Sides)]

    def body(*refs):
        refs = list(refs)
        buffers = refs[len(refs) - len(pairs) :]
        own = refs[len(flat_in) + len(flat_out) : len(refs) - len(pairs)]
        seen, after = [], []
        for j, kind in enumerate(kinds):
            if not isinstance(kind, Sides):
                seen.append(refs.pop(0))
                continue
            near, far, buffer = refs.pop(0), refs.pop(0), buffers.pop(0)
            odd = lax.rem(lax.axis_index(kind.axis), 2)
            if j < len(args):
                buffer[1 - odd] = near[...]
                buffer[odd] = far[...]
            else:
                after.append((near, far, buffer, odd))
            seen += [buffer.at[0], buffer.at[1]]
        kernel(*seen, *own)
        for near, far, buffer, odd in after:
            near[...] = buffer[1 - odd]
            far[...] = buffer[odd]

    results = pl.pallas_call(
        body,
        out_shape=flat_out,
        in_specs=[smem] * scalars + [vmem] * (len(flat_in) - scalars),
        out_specs=[vmem] * len(flat_out),
        scratch_shapes=[pltpu.VMEM(shape, f32) for shape in (*scratch, *pairs)],
        compiler_params=pltpu.CompilerParams(vmem_limit_bytes=40 * 2**20),
    )(*flat_in)
    results = list(results)
    out = []
    for kind in outs:
        if isinstance(kind, Sides):
            out.append(Sides(kind.axis, results.pop(0), results.pop(0)))
        else:
            out.append(results.pop(0))
    return out


def trade(sides):
    n = lax.axis_size(sides.axis)
    assert n % 2 == 0
    far = lax.ppermute(
        sides.far, sides.axis, [(i, (i + 1 if i % 2 else i - 1) % n) for i in range(n)]
    )
    near = lax.ppermute(sides.near, sides.axis, [(i, i - 1 if i % 2 else i + 1) for i in range(n)])
    return Sides(sides.axis, near, far)


def turn_round(message, axis):
    n = lax.axis_size(axis)
    below = lax.ppermute(message, axis, [(i, (i + 1) % n) for i in range(n)])
    if n == 2:
        return below, below
    above = lax.ppermute(message, axis, [((i + 1) % n, i) for i in range(n)])
    return below, above


def local(phase, displacement, slot_ids, grain_variant, variant_strain):
    ph = phase.reshape(-1, LANES)
    dp = displacement.reshape(-1, LANES)
    ids = slot_ids.reshape(SLOTS, -1)
    packed = jax.ShapeDtypeStruct((2, SLOTS, BLK, LANES), f32)
    padded = (SLOTS, BLK + 2, 32, LANES)
    square = (BLK, BLK, LANES)
    turned = (2, SLOTS, BLK, LANES)
    wide = jax.ShapeDtypeStruct((3, WIDE, WIDE, LANES), f32)
    double = (2, 3, WIDE, WIDE, LANES)
    extended = (2, WIDE, WIDE, LANES)

    part = rows_of(FACE)
    *parts, pk = call(faces_kernel, (part, part, part, part, rows_of(ZD), packed), (ph,))
    xs, ys, zm = call(
        start_kernel,
        (both("gx", SIDE), both("gy", SIDE), rows_of(ZD + 3 * BLK + SLOTS)),
        (dp, ids, *parts),
    )
    zl, zr = turn_round(zm, "gz")
    ys = trade(ys)
    xs = trade(xs)
    dys, ends = call(
        move_rows_kernel,
        (both("gy", 3 * BLK * REACH + 16), jax.ShapeDtypeStruct((3, BLK, LANES), f32)),
        (dp, zl, zr),
    )
    dys = trade(dys)
    phases, eigen, pk, zm, ys, mk, st = call(
        first_kernel,
        (
            rows_of(SLOTS * PLANE),
            rows_of(PLANE),
            packed,
            rows_of(ZD + BLK),
            both("gy", FACE + BLK * REACH),
            jax.ShapeDtypeStruct((6, SLOTS, SLOTS, LANES), f32),
            rows_of(SLOTS),
        ),
        (ids, grain_variant, variant_strain, ids, ph, dp, pk, xs, ys, zl, zr),
        scratch=(padded, square, turned, (SLOTS, LANES)),
        scalars=3,
    )
    zl, zr = turn_round(zm, "gz")
    ys = trade(ys)
    dxs, tall = call(
        move_layers_kernel,
        (both("gx", (3 * REACH + 3) * WIDE), jax.ShapeDtypeStruct((3, WIDE, LANES), f32)),
        (dp, dys, ends),
    )
    dxs = trade(dxs)
    eys, ends = call(strain_rows_kernel, (both("gy", 8), rows_of(BLK)), (zl, zr))
    eys = trade(eys)
    main, wing = call(spread_kernel, (wide, wide), (dp, dys, tall, dxs))
    xs, tall = call(
        strain_layers_kernel,
        (both("gx", FACE + (REACH + 1) * WIDE), rows_of(WIDE)),
        (eigen, phases, ys, eys, ends),
    )
    xs = trade(xs)

    phases, eigen, main, wing, xs, ys, zm = call(
        second_kernel,
        (
            rows_of(SLOTS * PLANE),
            rows_of(PLANE),
            wide,
            wide,
            both("gx", SWEEPS * BLK),
            both("gy", SWEEPS * BLK),
            rows_of(BLK),
        ),
        (main, wing, eigen, eys, tall, phases, pk, mk, st, xs, ys, zl, zr),
        scratch=(extended, double, padded, square, turned),
    )
    ys = trade(ys)
    xs = trade(xs)
    zl, zr = turn_round(zm, "gz")
    xes, zm = call(edges_kernel, (both("gx", BLK + 8), rows_of(8)), (ys, zl, zr))
    xes = trade(xes)
    zel, zer = turn_round(zm, "gz")
    (moved,) = call(
        last_kernel,
        (rows_of(3 * PLANE),),
        (main, wing, eigen, xs, ys, zl, zr, xes, zel, zer),
        scratch=(extended, double),
    )
    return phases.reshape(phase.shape), moved.reshape(displacement.shape)


def solution(mesh):
    spec = P(None, "gx", "gy", "gz")
    return jax.shard_map(
        local,
        mesh=mesh,
        in_specs=(spec, spec, spec, P(), P()),
        out_specs=(spec, spec),
        check_vma=False,
    )
```

```python
import dataclasses

import jax
import jax.numpy as jnp
from jax import lax
from jax.experimental import pallas as pl
from jax.experimental.pallas import tpu as pltpu
from jax.sharding import PartitionSpec as P


SLOTS = 8
BLK = 16
SWEEPS = 2

well_linear = 1.0
well_cubic = 1.0
cross_term = 1.5
gradient_energy = 2.0
time_step = 0.04
shear = 1.0
lame_first = 1.0
relax_step = 0.06
bulk_trace = 3.0 * lame_first + 2.0 * shear

LANES = 128
PLANE = BLK * BLK
REACH = 2 * SWEEPS
WIDE = BLK + 2 * REACH
GROUP = 2 * REACH
FACE = SLOTS * BLK
SIDE = FACE + BLK + SLOTS
XPHASE = (3 * REACH + 1) * WIDE
ZD = FACE // 2

f32 = jnp.float32


def lane_of(shape):
    return lax.broadcasted_iota(jnp.int32, shape, len(shape) - 1)


def roll(value, shift):
    if isinstance(shift, int):
        shift = shift % LANES
        if shift == 0:
            return value
    else:
        shift = lax.rem(shift + 2 * LANES, LANES)
    return pltpu.roll(value, shift, axis=value.ndim - 1)


def grow(ids):
    lane = lane_of((SLOTS, LANES)) // BLK
    out = jnp.zeros((SLOTS, LANES), f32)
    values = ids.astype(f32)
    for b in range(LANES // BLK):
        out = jnp.where(lane == b, jnp.broadcast_to(values[:, b : b + 1], (SLOTS, LANES)), out)
    return out


def faces_kernel(ph, xlo, xhi, ylo, yhi, zm, pk):
    for s in range(SLOTS):
        rows = pl.ds(s * BLK, BLK)
        xlo[rows, :] = ph[pl.ds(s * PLANE, BLK), :]
        xhi[rows, :] = ph[pl.ds(s * PLANE + PLANE - BLK, BLK), :]
        ylo[rows, :] = ph[pl.ds(s * PLANE, BLK, stride=BLK), :]
        yhi[rows, :] = ph[pl.ds(s * PLANE + BLK - 1, BLK, stride=BLK), :]
    pack_seams(ph, pk)
    for s in range(SLOTS):
        zm[pl.ds(s * 8, 8), :] = fold_seams(pk, s)


def pack_seams(phases, pk):
    seam = seam_of((8, LANES))
    for s in range(SLOTS):
        for half in range(2):
            for odd in range(2):
                seams = jnp.zeros((8, LANES), f32)
                for k in range(BLK // 2):
                    value = phases[pl.ds(s * PLANE + (2 * k + odd) * BLK + 8 * half, 8), :]
                    seams = jnp.where(seam == k, roll(value, 2 * k), seams)
                pk[odd, s, pl.ds(8 * half, 8), :] = seams


def seam_of(shape):
    return (lane_of(shape) + 1) % BLK // 2


def fold_seams(pk, s):
    lane = (lane_of((8, LANES)) + 1) % LANES // BLK
    out = jnp.zeros((8, LANES), f32)
    for c, (half, odd) in enumerate(((0, 0), (0, 1), (1, 0), (1, 1))):
        out = jnp.where(lane == c, roll(pk[odd, s, pl.ds(8 * half, 8), :], BLK * c), out)
    return out


def start_kernel(dp, ids, *refs):
    for source, ref in zip(refs[:5], refs[5:]):
        rows = pl.ds(0, source.shape[0])
        ref[rows, :] = source[...]
    xlo, xhi, ylo, yhi, zm = refs[5:]
    numbers = grow(ids[...])
    rows = pl.ds(FACE, BLK)
    xlo[rows, :] = dp[pl.ds(0, BLK), :]
    xhi[rows, :] = dp[pl.ds(PLANE - BLK, BLK), :]
    ylo[rows, :] = dp[pl.ds(PLANE, BLK, stride=BLK), :]
    yhi[rows, :] = dp[pl.ds(PLANE + BLK - 1, BLK, stride=BLK), :]
    for ref in (xlo, xhi, ylo, yhi):
        ref[pl.ds(FACE + BLK, SLOTS), :] = numbers
    zm[pl.ds(ZD + 3 * BLK, SLOTS), :] = numbers
    for f in range(3):
        zm[pl.ds(ZD + f * BLK, BLK), :] = pack_ends(
            lambda x: dp[pl.ds(f * PLANE + x * BLK, BLK), :], BLK
        )


def pack_ends(layer, rows):
    spot = lane_of((rows, LANES)) // GROUP
    out = jnp.zeros((rows, LANES), f32)
    for x in range(BLK):
        out = jnp.where(spot == x, roll(layer(x), GROUP * x + REACH), out)
    return out


def unpack_ends(packed, x):
    return roll(packed, -(GROUP * x + REACH))


def join_ends(left, right):
    return jnp.where(lane_of(left.shape) % GROUP >= REACH, right, left)


def update_phases(load, pp, mk, st, faces, pk, dil, out, e_out, mv):
    xm, xp, ym, yp, zl, zr = faces
    lane = lane_of((8, LANES))
    spot = lane % BLK

    def fill(x, _):
        for s in range(SLOTS):
            pp[s, x + 1, pl.ds(8, BLK), :] = load(s, x)
        return 0

    lax.fori_loop(0, BLK, fill, 0, unroll=True)

    def match(direction, s, layers):
        total = None
        for t in range(SLOTS):
            term = mk[direction, s, pl.ds(t, 1), :] * layers[t]
            total = term if total is None else total + term
        return total

    for direction, face, place in ((0, xm, 0), (1, xp, BLK + 1)):
        layers = [face(t) for t in range(SLOTS)]
        for s in range(SLOTS):
            pp[s, place, pl.ds(8, BLK), :] = match(direction, s, layers)
    for direction, face, place in ((2, ym, 7), (3, yp, 8 + BLK)):
        layers = [face(t) for t in range(SLOTS)]
        for s in range(SLOTS):
            moved = match(direction, s, layers)
            for x in range(BLK):
                pp[s, x + 1, pl.ds(place, 1), :] = moved[x : x + 1, :]
    border = (lane + 1) % LANES < BLK
    upper = lane % 2 == 0
    for half in range(2):
        rows = pl.ds(8 * half, 8)
        for odd in range(2):
            c = 2 * half + odd
            layers = []
            for t in range(SLOTS):
                seams = pk[odd, t, rows, :]
                below = jnp.where(border, roll(zl(t), -BLK * c), seams)
                above = jnp.where(border, roll(zr(t), -BLK * c), seams)
                layers.append(jnp.where(upper, roll(below, 1), roll(above, -1)))
            for s in range(SLOTS):
                mv[odd, s, rows, :] = match(4, s, layers)

    def layers(k, _):
        for odd, half in ((0, 0), (0, 1), (1, 0), (1, 1)):
            x = 2 * k + odd
            r0 = 8 + 8 * half
            rows = pl.ds(8 * half, 8)
            values = [pp[s, x + 1, pl.ds(r0, 8), :] for s in range(SLOTS)]
            total = None
            eigen = None
            for s in range(SLOTS):
                square = values[s] * values[s]
                part = square * st[pl.ds(s, 1), :]
                total = square if total is None else total + square
                eigen = part if eigen is None else eigen + part
            trace = bulk_trace * (dil[x, rows, :] - 3.0 * eigen)
            base = (1.0 + time_step * well_linear - 6.0 * time_step * gradient_energy) - (
                2.0 * cross_term * time_step
            ) * total
            pull = (2.0 * time_step) * trace
            fresh = None
            for s in range(SLOTS):
                p = values[s]
                seams = roll(mv[odd, s, rows, :], -2 * k)
                after = jnp.where(spot == BLK - 1, seams, roll(p, -1))
                before = jnp.where(spot == 0, seams, roll(p, 1))
                near = (
                    (pp[s, x, pl.ds(r0, 8), :] + pp[s, x + 2, pl.ds(r0, 8), :])
                    + (pp[s, x + 1, pl.ds(r0 - 1, 8), :] + pp[s, x + 1, pl.ds(r0 + 1, 8), :])
                    + (after + before)
                )
                rate = (
                    base
                    + (time_step * (2.0 * cross_term - well_cubic)) * (p * p)
                    + pull * st[pl.ds(s, 1), :]
                )
                new = p * rate + (time_step * gradient_energy) * near
                out[pl.ds(pl.multiple_of(s * PLANE + x * BLK + 8 * half, 8), 8), :] = new
                part = new * new * st[pl.ds(s, 1), :]
                fresh = part if fresh is None else fresh + part
            e_out[pl.ds(pl.multiple_of(x * BLK + 8 * half, 8), 8), :] = fresh
        return 0

    lax.fori_loop(0, BLK // 2, layers, 0)


def first_kernel(
    ids_s, variant_s, strain_s, ids, ph, dp, pk, xm, xp, ym, yp, zl, zr,
    out, e_out, pk_out, zm, ylo, yhi, mk, st, pp, dil, mv, act,
):
    grains = variant_s.shape[0]
    own = grow(ids[...])
    lane = lane_of((SLOTS, LANES))
    owner = lane_of((1, LANES)) // BLK
    for s in range(SLOTS):
        row = jnp.zeros((1, LANES), f32)
        live = jnp.zeros((1, LANES), f32)
        for b in range(LANES // BLK):
            number = ids_s[s, b]
            value = strain_s[variant_s[jnp.minimum(number, grains - 1)]]
            row = jnp.where(owner == b, jnp.where(number < grains, value, 0.0), row)
            live = jnp.where(owner == b, jnp.where(number < grains, 1.0, 0.0), live)
        st[pl.ds(s, 1), :] = row
        act[pl.ds(s, 1), :] = live
    tail = pl.ds(FACE + BLK, SLOTS)
    ztail = pl.ds(ZD + 3 * BLK, SLOTS)
    beside = [xm[tail, :], xp[tail, :], ym[tail, :], yp[tail, :]]
    even = lane % 2 == 0
    below = jnp.where(lane < BLK, roll(zl[ztail, :], BLK), roll(own, BLK))
    above = roll(jnp.where(lane < BLK, zr[ztail, :], own), -1)
    beside.append(jnp.where(even, below, above))
    owners = [own] * 4 + [jnp.where(even, own, roll(own, BLK - 1))]
    for direction in range(5):
        for s in range(SLOTS):
            mine = owners[direction][s : s + 1, :]
            mk[direction, s] = jnp.where(
                (mine == beside[direction]) & (mine < float(grains)), 1.0, 0.0
            )

    lane2 = lane_of((BLK, LANES))
    row2 = lax.broadcasted_iota(jnp.int32, (BLK, LANES), 0)
    urow = pl.ds(FACE, BLK)
    wrow = pl.ds(ZD + 2 * BLK, BLK)
    ends = join_ends(zl[wrow, :], zr[wrow, :])
    for x in range(BLK):
        up = xp[urow, :] if x == BLK - 1 else dp[pl.ds((x + 1) * BLK, BLK), :]
        down = xm[urow, :] if x == 0 else dp[pl.ds((x - 1) * BLK, BLK), :]
        v = dp[pl.ds(PLANE + x * BLK, BLK), :]
        vp = jnp.where(row2 == BLK - 1, yp[pl.ds(FACE + x, 1), :], pltpu.roll(v, BLK - 1, axis=0))
        vm = jnp.where(row2 == 0, ym[pl.ds(FACE + x, 1), :], pltpu.roll(v, 1, axis=0))
        w = dp[pl.ds(2 * PLANE + x * BLK, BLK), :]
        edge = unpack_ends(ends, x)
        dil[x] = 0.5 * ((up - down) + (vp - vm) + (shift_z(w, edge, 1) - shift_z(w, edge, -1)))

    def load(s, x):
        rows = pl.ds(pl.multiple_of(s * PLANE + x * BLK, BLK), BLK)
        return ph[rows, :] * act[pl.ds(s, 1), :]

    faces = (
        lambda t: xm[pl.ds(t * BLK, BLK), :],
        lambda t: xp[pl.ds(t * BLK, BLK), :],
        lambda t: ym[pl.ds(t * BLK, BLK), :],
        lambda t: yp[pl.ds(t * BLK, BLK), :],
        lambda t: zl[pl.ds(t * 8, 8), :],
        lambda t: zr[pl.ds(t * 8, 8), :],
    )
    update_phases(load, pp, mk, st, faces, pk, dil, out, e_out, mv)
    pack_seams(out, pk_out)
    for s in range(SLOTS):
        zm[pl.ds(s * 8, 8), :] = fold_seams(pk_out, s)
        rows = pl.ds(s * BLK, BLK)
        ylo[rows, :] = out[pl.ds(s * PLANE, BLK, stride=BLK), :]
        yhi[rows, :] = out[pl.ds(s * PLANE + BLK - 1, BLK, stride=BLK), :]
    zm[pl.ds(ZD, BLK), :] = pack_ends(lambda x: e_out[pl.ds(x * BLK, BLK), :], BLK)
    y_sides(e_out, REACH, FACE, ylo, yhi)


def y_sides(e, halo, base, ylo, yhi):
    for x in range(BLK):
        rows = pl.ds(base + x * halo, halo)
        ylo[rows, :] = e[pl.ds(x * BLK, halo), :]
        yhi[rows, :] = e[pl.ds(x * BLK + BLK - halo, halo), :]


def move_rows_kernel(dp, zl, zr, ylo, yhi, ends):
    for f in range(3):
        rows = pl.ds(ZD + f * BLK, BLK)
        ends[f] = join_ends(zl[rows, :], zr[rows, :])
        for x in range(BLK):
            place = pl.ds((f * BLK + x) * REACH, REACH)
            start = f * PLANE + x * BLK
            ylo[place, :] = dp[pl.ds(start, REACH), :]
            yhi[place, :] = dp[pl.ds(start + BLK - REACH, REACH), :]
        place = pl.ds(3 * BLK * REACH + f * REACH, REACH)
        ylo[place, :] = ends[f, pl.ds(0, REACH), :]
        yhi[place, :] = ends[f, pl.ds(BLK - REACH, REACH), :]


def move_layers_kernel(dp, ym, yp, ends, ph, xlo, xhi, tall):
    inner = pl.ds(REACH, BLK)
    for f in range(3):
        side = pl.ds(3 * BLK * REACH + f * REACH, REACH)
        tall[f, pl.ds(0, REACH), :] = ym[side, :]
        tall[f, inner, :] = ends[f]
        tall[f, pl.ds(REACH + BLK, REACH), :] = yp[side, :]
        for ref, first in ((xlo, 0), (xhi, BLK - REACH)):
            for k in range(REACH):
                x = first + k
                base = (f * REACH + k) * WIDE
                side = pl.ds((f * BLK + x) * REACH, REACH)
                ref[pl.ds(base, REACH), :] = ym[side, :]
                ref[pl.ds(base + REACH, BLK), :] = dp[pl.ds(f * PLANE + x * BLK, BLK), :]
                ref[pl.ds(base + REACH + BLK, REACH), :] = yp[side, :]
    block = GROUP * REACH
    third = lane_of((WIDE, LANES)) // block
    for ref, x, turn in ((xlo, 0, 0), (xhi, BLK - 1, block)):
        ends_of = [roll(tall[f], f * block + turn) for f in range(3)]
        ref[pl.ds(3 * REACH * WIDE, WIDE), :] = jnp.where(
            third == 0, ends_of[0], jnp.where(third == 1, ends_of[1], ends_of[2])
        )
        for s in range(SLOTS):
            ref[pl.ds(XPHASE + s * BLK, BLK), :] = ph[pl.ds(s * PLANE + x * BLK, BLK), :]


def spread_kernel(dp, ym, yp, tall, xm, xp, main, wing):
    for f in range(3):
        for x in range(BLK):
            side = pl.ds((f * BLK + x) * REACH, REACH)
            i = x + REACH
            main[f, i, pl.ds(0, REACH), :] = ym[side, :]
            main[f, i, pl.ds(REACH, BLK), :] = dp[pl.ds(f * PLANE + x * BLK, BLK), :]
            main[f, i, pl.ds(REACH + BLK, REACH), :] = yp[side, :]
            wing[f, i] = unpack_ends(tall[f], x)
        ends = pl.ds(3 * REACH * WIDE, WIDE)
        for k in range(REACH):
            rows = pl.ds((f * REACH + k) * WIDE, WIDE)
            main[f, k] = xm[rows, :]
            main[f, REACH + BLK + k] = xp[rows, :]
            wing[f, k] = unpack_ends(xm[ends, :], f * REACH + k)
            wing[f, REACH + BLK + k] = unpack_ends(xp[ends, :], f * REACH + k)


def strain_rows_kernel(zl, zr, ylo, yhi, ends):
    rows = pl.ds(ZD, BLK)
    joined = join_ends(zl[rows, :], zr[rows, :])
    ends[...] = joined
    ylo[...] = joined[:8, :]
    yhi[...] = joined[BLK - 8 :, :]


def strain_layers_kernel(e, ym, yp, em, ep, ends, xlo, xhi, tall):
    tall[pl.ds(0, REACH), :] = em[pl.ds(8 - REACH, REACH), :]
    tall[pl.ds(REACH, BLK), :] = ends[...]
    tall[pl.ds(REACH + BLK, REACH), :] = ep[pl.ds(0, REACH), :]
    for ref, first in ((xlo, 0), (xhi, BLK - REACH)):
        for k in range(REACH):
            x = first + k
            base = k * WIDE
            side = pl.ds(FACE + x * REACH, REACH)
            ref[pl.ds(base, REACH), :] = ym[side, :]
            ref[pl.ds(base + REACH, BLK), :] = e[pl.ds(x * BLK, BLK), :]
            ref[pl.ds(base + REACH + BLK, REACH), :] = yp[side, :]
        ref[pl.ds(REACH * WIDE, WIDE), :] = tall[...]


def shift_z(main, wing, sign):
    edge = lane_of(main.shape) == (0 if sign > 0 else LANES - 1)
    return roll(jnp.where(edge, wing, main), -sign)


def sweep(src, e, write, first, stop, windows, outer):
    turn = 0.5 * (lame_first + shear) * 0.5
    bulk = 0.5 * bulk_trace
    own = shear + (lame_first + shear)
    keep = 1.0 - relax_step * (6.0 * shear + 2.0 * (lame_first + shear))

    def layer(i, _):
        for r in windows:
            here, ups, downs = [], [], []
            for tile in range(2):
                u, v, w = [src(tile, k, i, r) for k in range(3)]
                gx = turn * (src(tile, 2, i + 1, r) - src(tile, 2, i - 1, r))
                gy = turn * (src(tile, 2, i, r + 1) - src(tile, 2, i, r - 1))
                gz = turn * (
                    (src(tile, 0, i + 1, r) - src(tile, 0, i - 1, r))
                    + (src(tile, 1, i, r + 1) - src(tile, 1, i, r - 1))
                ) - bulk * e(tile, i, r)
                wide = own * w
                here.append((u, v, w))
                ups.append((u + gx, v + gy, wide + gz))
                downs.append((u - gx, v - gy, wide - gz))
            for tile in range(2):
                for k in range(3):
                    if tile and k not in outer:
                        continue
                    lane_part = shift_z(ups[tile][k], ups[1 - tile][k], 1) + shift_z(
                        downs[tile][k], downs[1 - tile][k], -1
                    )
                    x_part = src(tile, k, i + 1, r) + src(tile, k, i - 1, r)
                    y_part = src(tile, k, i, r + 1) + src(tile, k, i, r - 1)
                    if k < 2:
                        o = 1 - k
                        cross = (src(tile, o, i + 1, r + 1) - src(tile, o, i + 1, r - 1)) - (
                            src(tile, o, i - 1, r + 1) - src(tile, o, i - 1, r - 1)
                        )
                        if k == 0:
                            slope = e(tile, i + 1, r) - e(tile, i - 1, r)
                            near = own * x_part + y_part
                        else:
                            slope = e(tile, i, r + 1) - e(tile, i, r - 1)
                            near = own * y_part + x_part
                        change = near + lane_part + (turn * cross - bulk * slope)
                    else:
                        change = (x_part + y_part) + lane_part
                    write(tile, k, i, r, keep * here[tile][k] + relax_step * change)
        return 0

    lax.fori_loop(first, stop, layer, 0, unroll=True)


def relax(halo, main, wing, e, mid, write, outer):
    low, high = REACH - halo + 1, REACH + BLK + halo - 1

    def spans(low, high):
        return sorted({min(r, high - 8) for r in range(low, high, 8)})

    fields = (main, wing)

    def load(tile, k, i, r):
        return fields[tile][k, i, pl.ds(r, 8), :]

    def load_mid(tile, k, i, r):
        return mid[tile, k, i, pl.ds(r, 8), :]

    def load_e(tile, i, r):
        return e[tile, i, pl.ds(r, 8), :]

    def write_mid(tile, k, i, r, value):
        mid[tile, k, i, pl.ds(r, 8), :] = value

    sweep(load, load_e, write_mid, low, high, spans(low, high), (0, 1, 2))
    sweep(load_mid, load_e, write, low + 1, high - 1, spans(low + 1, high - 1), outer)


def second_kernel(
    main, wing, e_in, eym, eyp, tall, ph, pk, mk, st, exm, exp, xm, xp, ym, yp, zl, zr,
    out, e_out, moved, aside, xlo, xhi, ylo, yhi, zm, e, mid, pp, dil, mv,
):
    for x in range(BLK):
        i = x + REACH
        side = pl.ds(FACE + x * REACH, REACH)
        e[0, i, pl.ds(0, REACH), :] = ym[side, :]
        e[0, i, pl.ds(REACH, BLK), :] = e_in[pl.ds(x * BLK, BLK), :]
        e[0, i, pl.ds(REACH + BLK, REACH), :] = yp[side, :]
        e[1, i] = unpack_ends(tall[...], x)
    ends = pl.ds(REACH * WIDE, WIDE)
    for k in range(REACH):
        rows = pl.ds(k * WIDE, WIDE)
        e[0, k] = exm[rows, :]
        e[0, REACH + BLK + k] = exp[rows, :]
        e[1, k] = unpack_ends(exm[ends, :], BLK - REACH + k)
        e[1, REACH + BLK + k] = unpack_ends(exp[ends, :], k)

    results = (moved, aside)

    def write(tile, k, i, r, value):
        results[tile][k, i, pl.ds(r, 8), :] = value

    relax(REACH, main, wing, e, mid, write, (0, 1, 2))

    def strain_rate(x, _):
        i = x + REACH
        for half in range(2):
            r = REACH + 8 * half
            rows = pl.ds(r, 8)
            w, side = moved[2, i, rows, :], aside[2, i, rows, :]
            dil[x, pl.ds(8 * half, 8), :] = 0.5 * (
                (moved[0, i + 1, rows, :] - moved[0, i - 1, rows, :])
                + (moved[1, i, pl.ds(r + 1, 8), :] - moved[1, i, pl.ds(r - 1, 8), :])
                + (shift_z(w, side, 1) - shift_z(w, side, -1))
            )
        return 0

    lax.fori_loop(0, BLK, strain_rate, 0, unroll=True)

    def load(s, x):
        return ph[pl.ds(pl.multiple_of(s * PLANE + x * BLK, BLK), BLK), :]

    faces = (
        lambda t: xm[pl.ds(XPHASE + t * BLK, BLK), :],
        lambda t: xp[pl.ds(XPHASE + t * BLK, BLK), :],
        lambda t: ym[pl.ds(t * BLK, BLK), :],
        lambda t: yp[pl.ds(t * BLK, BLK), :],
        lambda t: zl[pl.ds(t * 8, 8), :],
        lambda t: zr[pl.ds(t * 8, 8), :],
    )
    update_phases(load, pp, mk, st, faces, pk, dil, out, e_out, mv)
    for k in range(SWEEPS):
        xlo[pl.ds(k * BLK, BLK), :] = e_out[pl.ds(k * BLK, BLK), :]
        xhi[pl.ds(k * BLK, BLK), :] = e_out[pl.ds((BLK - SWEEPS + k) * BLK, BLK), :]
    y_sides(e_out, SWEEPS, 0, ylo, yhi)
    zm[...] = pack_ends(lambda x: e_out[pl.ds(x * BLK, BLK), :], BLK)


def edges_kernel(ym, yp, zl, zr, xlo, xhi, zm):
    joined = join_ends(zl[...], zr[...])
    for ref, first in ((xlo, 0), (xhi, BLK - SWEEPS)):
        ref[pl.ds(0, BLK), :] = joined
        for k in range(SWEEPS):
            side = pl.ds((first + k) * SWEEPS, SWEEPS)
            ref[pl.ds(BLK + k * SWEEPS, SWEEPS), :] = ym[side, :]
            ref[pl.ds(BLK + (SWEEPS + k) * SWEEPS, SWEEPS), :] = yp[side, :]

    def rows(x):
        side = pl.ds(x * SWEEPS, SWEEPS)
        blank = jnp.zeros((8 - 2 * SWEEPS, LANES), f32)
        return jnp.concatenate([ym[side, :], yp[side, :], blank], axis=0)

    zm[...] = pack_ends(rows, 8)


def last_kernel(
    main, wing, e_in, xm, xp, ym, yp, zl, zr, xem, xep, zel, zer, out, e, mid
):
    n = SWEEPS
    before, after = REACH - n, REACH + BLK
    own = pl.ds(REACH, BLK)
    joined = join_ends(zl[...], zr[...])
    edges = join_ends(zel[...], zer[...])
    for x in range(BLK):
        i = x + REACH
        side = pl.ds(x * n, n)
        e[0, i, pl.ds(before, n), :] = ym[side, :]
        e[0, i, own, :] = e_in[pl.ds(x * BLK, BLK), :]
        e[0, i, pl.ds(after, n), :] = yp[side, :]
        e[1, i, own, :] = unpack_ends(joined, x)
        turned = unpack_ends(edges, x)
        e[1, i, pl.ds(before, n), :] = turned[:n, :]
        e[1, i, pl.ds(after, n), :] = turned[n : 2 * n, :]
    for k in range(n):
        rows = pl.ds(k * BLK, BLK)
        for flat, edge, i, x in ((xm, xem, before + k, BLK - n + k), (xp, xep, after + k, k)):
            e[0, i, own, :] = flat[rows, :]
            e[0, i, pl.ds(before, n), :] = edge[pl.ds(BLK + k * n, n), :]
            e[0, i, pl.ds(after, n), :] = edge[pl.ds(BLK + (n + k) * n, n), :]
            e[1, i, own, :] = unpack_ends(edge[pl.ds(0, BLK), :], x)

    def write(tile, k, i, r, value):
        place = k * PLANE + (i - REACH) * BLK + (r - REACH)
        out[pl.ds(place if isinstance(place, int) else pl.multiple_of(place, 8), 8), :] = value

    relax(n, main, wing, e, mid, write, ())


def rows_of(n):
    return jax.ShapeDtypeStruct((n, LANES), f32)


@dataclasses.dataclass(frozen=True)
class Sides:
    axis: str
    near: object
    far: object


def both(axis, rows):
    return Sides(axis, rows_of(rows), rows_of(rows))


def call(kernel, outs, args, scratch=(), scalars=0):
    vmem = pl.BlockSpec(memory_space=pltpu.VMEM)
    smem = pl.BlockSpec(memory_space=pltpu.SMEM)
    kinds = [*args, *outs]
    flat_in = [part for a in args for part in ((a.near, a.far) if isinstance(a, Sides) else (a,))]
    flat_out = [part for a in outs for part in ((a.near, a.far) if isinstance(a, Sides) else (a,))]
    pairs = [(2,) + a.near.shape for a in kinds if isinstance(a, Sides)]

    def body(*refs):
        refs = list(refs)
        buffers = refs[len(refs) - len(pairs) :]
        own = refs[len(flat_in) + len(flat_out) : len(refs) - len(pairs)]
        seen, after = [], []
        for j, kind in enumerate(kinds):
            if not isinstance(kind, Sides):
                seen.append(refs.pop(0))
                continue
            near, far, buffer = refs.pop(0), refs.pop(0), buffers.pop(0)
            odd = lax.rem(lax.axis_index(kind.axis), 2)
            if j < len(args):
                buffer[1 - odd] = near[...]
                buffer[odd] = far[...]
            else:
                after.append((near, far, buffer, odd))
            seen += [buffer.at[0], buffer.at[1]]
        kernel(*seen, *own)
        for near, far, buffer, odd in after:
            near[...] = buffer[1 - odd]
            far[...] = buffer[odd]

    results = pl.pallas_call(
        body,
        out_shape=flat_out,
        in_specs=[smem] * scalars + [vmem] * (len(flat_in) - scalars),
        out_specs=[vmem] * len(flat_out),
        scratch_shapes=[pltpu.VMEM(shape, f32) for shape in (*scratch, *pairs)],
        compiler_params=pltpu.CompilerParams(vmem_limit_bytes=40 * 2**20),
    )(*flat_in)
    results = list(results)
    out = []
    for kind in outs:
        if isinstance(kind, Sides):
            out.append(Sides(kind.axis, results.pop(0), results.pop(0)))
        else:
            out.append(results.pop(0))
    return out


def trade(sides):
    n = lax.axis_size(sides.axis)
    assert n % 2 == 0
    far = lax.ppermute(
        sides.far, sides.axis, [(i, (i + 1 if i % 2 else i - 1) % n) for i in range(n)]
    )
    near = lax.ppermute(sides.near, sides.axis, [(i, i - 1 if i % 2 else i + 1) for i in range(n)])
    return Sides(sides.axis, near, far)


def turn_round(message, axis):
    n = lax.axis_size(axis)
    below = lax.ppermute(message, axis, [(i, (i + 1) % n) for i in range(n)])
    if n == 2:
        return below, below
    above = lax.ppermute(message, axis, [((i + 1) % n, i) for i in range(n)])
    return below, above


def local(phase, displacement, slot_ids, grain_variant, variant_strain):
    ph = phase.reshape(-1, LANES)
    dp = displacement.reshape(-1, LANES)
    ids = slot_ids.reshape(SLOTS, -1)
    packed = jax.ShapeDtypeStruct((2, SLOTS, BLK, LANES), f32)
    padded = (SLOTS, BLK + 2, 32, LANES)
    square = (BLK, BLK, LANES)
    turned = (2, SLOTS, BLK, LANES)
    wide = jax.ShapeDtypeStruct((3, WIDE, WIDE, LANES), f32)
    double = (2, 3, WIDE, WIDE, LANES)
    extended = (2, WIDE, WIDE, LANES)

    part = rows_of(FACE)
    *parts, pk = call(faces_kernel, (part, part, part, part, rows_of(ZD), packed), (ph,))
    xs, ys, zm = call(
        start_kernel,
        (both("gx", SIDE), both("gy", SIDE), rows_of(ZD + 3 * BLK + SLOTS)),
        (dp, ids, *parts),
    )
    zl, zr = turn_round(zm, "gz")
    ys = trade(ys)
    xs = trade(xs)
    dys, ends = call(
        move_rows_kernel,
        (both("gy", 3 * BLK * REACH + 16), jax.ShapeDtypeStruct((3, BLK, LANES), f32)),
        (dp, zl, zr),
    )
    dys = trade(dys)
    phases, eigen, pk, zm, ys, mk, st = call(
        first_kernel,
        (
            rows_of(SLOTS * PLANE),
            rows_of(PLANE),
            packed,
            rows_of(ZD + BLK),
            both("gy", FACE + BLK * REACH),
            jax.ShapeDtypeStruct((5, SLOTS, SLOTS, LANES), f32),
            rows_of(SLOTS),
        ),
        (ids, grain_variant, variant_strain, ids, ph, dp, pk, xs, ys, zl, zr),
        scratch=(padded, square, turned, (SLOTS, LANES)),
        scalars=3,
    )
    zl, zr = turn_round(zm, "gz")
    ys = trade(ys)
    dxs, tall = call(
        move_layers_kernel,
        (both("gx", XPHASE + FACE), jax.ShapeDtypeStruct((3, WIDE, LANES), f32)),
        (dp, dys, ends, phases),
    )
    dxs = trade(dxs)
    eys, ends = call(strain_rows_kernel, (both("gy", 8), rows_of(BLK)), (zl, zr))
    eys = trade(eys)
    main, wing = call(spread_kernel, (wide, wide), (dp, dys, tall, dxs))
    xs, tall = call(
        strain_layers_kernel,
        (both("gx", (REACH + 1) * WIDE), rows_of(WIDE)),
        (eigen, ys, eys, ends),
    )
    exs = trade(xs)

    phases, eigen, main, wing, xs, ys, zm = call(
        second_kernel,
        (
            rows_of(SLOTS * PLANE),
            rows_of(PLANE),
            wide,
            wide,
            both("gx", SWEEPS * BLK),
            both("gy", SWEEPS * BLK),
            rows_of(BLK),
        ),
        (main, wing, eigen, eys, tall, phases, pk, mk, st, exs, dxs, ys, zl, zr),
        scratch=(extended, double, padded, square, turned),
    )
    ys = trade(ys)
    xs = trade(xs)
    zl, zr = turn_round(zm, "gz")
    xes, zm = call(edges_kernel, (both("gx", BLK + 8), rows_of(8)), (ys, zl, zr))
    xes = trade(xes)
    zel, zer = turn_round(zm, "gz")
    (moved,) = call(
        last_kernel,
        (rows_of(3 * PLANE),),
        (main, wing, eigen, xs, ys, zl, zr, xes, zel, zer),
        scratch=(extended, double),
    )
    return phases.reshape(phase.shape), moved.reshape(displacement.shape)


def solution(mesh):
    spec = P(None, "gx", "gy", "gz")
    return jax.shard_map(
        local,
        mesh=mesh,
        in_specs=(spec, spec, spec, P(), P()),
        out_specs=(spec, spec),
        check_vma=False,
    )
```
